32 devices in a mesh: seq: 8 (over y, x, core), red: 4 (over z).
Axes of the slice: x: 2, y: 2, z: 4, core: 2. Of those that a mesh axis runs over, the one named last changes fastest.
Arguments:
- token_ids: int32 [1024], P('seq'), may hold values from 0 to 511
- embedding: bfloat16 [512, 4096], P(None, 'red'), may hold values from -6 to 6
- proj_weight: bfloat16 [4096, 3, 4, 256], P('red', None, None, 'seq'), may hold values from -0.09375 to 0.09375
- filters: float32 [1024, 1024], P('seq', 'red'), may hold values from -1 to 1
- cotangent: float32 [1024, 1024], P('seq', 'red'), may hold values from -6 to 6
Outputs:
- output: float32 [1024, 1024], P('seq', 'red')
- filter_grad: float32 [1024, 1024], P('seq', 'red')
- branch_grads: bfloat16 [1024, 3, 1024], P('seq', None, 'red')
- weight_grad: float32 [4096, 3, 4, 256], P('red', None, None, 'seq')
The draws below stay inside these ranges and needn't reach their ends.
All inputs are finite; a program needn't handle non-finite values.
Results may differ from the reference program's by a relative error of at most 0.0029.
Values sent between devices are 32-bit elements; how exact they have to be, the bound alone decides.
A program may use at most 64 MiB of HBM per device.

```python
import math
import jax
import jax.numpy as jnp
from jax import lax

D = 4096
C = 1024
VOCAB = 512
TOKENS = 1024
N_RED = 4


def draw_filters(key, part):
    rate_key, pick_key, noise_key, fast_key = jax.random.split(key, 4)
    positions = jnp.arange(TOKENS, dtype=jnp.float32)[:, None]
    slow_rates = jnp.exp(jax.random.uniform(rate_key, (C,), jnp.float32, math.log(0.1 / TOKENS), math.log(2.3 / TOKENS)))
    fast_rates = jnp.exp(jax.random.uniform(fast_key, (C,), jnp.float32, math.log(2.3 / TOKENS), math.log(1.0 / 30.0)))
    picked = jax.random.uniform(pick_key, (C,), jnp.float32)
    keeping = picked < 0.5
    noise = jnp.clip(jax.random.normal(noise_key, (TOKENS, C), jnp.float32), -4.0, 4.0)
    rates = jnp.where(keeping, slow_rates, fast_rates)
    shaped = noise * jnp.exp(-positions * rates[None, :])
    return shaped * jax.lax.rsqrt(jnp.sum(shaped * shaped, axis=0, keepdims=True))


def touch_ends(array, stream_key, least, largest):
    index_at = [jax.random.randint(jax.random.fold_in(stream_key, axis), (), 0, length) for axis, length in enumerate(array.shape)]
    main_axis = array.shape.index(max(array.shape))
    beside = index_at[:main_axis] + [(index_at[main_axis] + 1) % array.shape[main_axis]] + index_at[main_axis + 1:]
    return array.at[tuple(index_at)].set(least).at[tuple(beside)].set(largest)


def steps_of(rng, shape, shards, low, largest):
    level, own = 1.0, jax.random.fold_in(rng, 6)
    for axis_at, blocks in shards:
        steps = jnp.exp(jax.random.uniform(jax.random.fold_in(own, axis_at), (blocks,), jnp.float32, low / len(shards), largest / len(shards)))
        level = level * jnp.repeat(steps, shape[axis_at] // blocks).reshape([-1 if axis == axis_at else 1 for axis in range(len(shape))])
    return level


def scatter_about(rng, dims, width, most, shards=(), kind=jnp.bfloat16):
    array = jax.random.normal(rng, dims, jnp.float32) * width
    if len(shards) > 0:
        array = steps_of(rng, dims, shards, -0.22, 0.18) * array
    return jnp.clip(array, min=-most, max=most).astype(kind)


def setup_inputs(seed: int = 0) -> dict:
    arg_keys = jax.random.split(jax.random.key(seed), 6)
    return {
        "token_ids": touch_ends(jax.random.randint(arg_keys[0], (TOKENS,), 0, VOCAB), jax.random.fold_in(arg_keys[0], 1), 0, VOCAB - 1).astype(jnp.int32),
        "embedding": scatter_about(arg_keys[1], (VOCAB, D), 1.0, 6.0, ((1, 4),)),
        "proj_weight": scatter_about(arg_keys[2], (D, 3, N_RED, C // N_RED), D ** -0.5, 0.09375, ((0, 4), (3, 8))),
        "filters": draw_filters(jax.random.fold_in(arg_keys[5], 71), 0),
        "cotangent": scatter_about(arg_keys[4], (TOKENS, C), 1.0, 6.0, ((0, 8), (1, 4)), jnp.float32),
    }


def reference(token_ids, embedding, proj_weight, filters, cotangent):
    weight_matrix = proj_weight.reshape(D, 3 * C)
    lookup = jnp.dot(embedding, weight_matrix, preferred_element_type=jnp.float32)
    projected = jnp.take(lookup, token_ids, axis=0)
    queries = projected[:, :C]
    key_rows = projected[:, C:2 * C]
    value_rows = projected[:, 2 * C:]
    inner = key_rows * value_rows
    upstream = cotangent * queries
    length = token_ids.shape[0]
    padded = 2 * length
    spectra = jnp.fft.rfft(jnp.concatenate([filters, inner, upstream], axis=1), n=padded, axis=0)
    filt_spec = spectra[:, :C]
    inner_spec = spectra[:, C:2 * C]
    up_spec = spectra[:, 2 * C:]
    joined = jnp.concatenate([filt_spec * inner_spec, jnp.conj(filt_spec) * up_spec, up_spec * jnp.conj(inner_spec)], axis=1)
    back = jnp.fft.irfft(joined, n=padded, axis=0)[:length]
    conv = back[:, :C]
    grad_inner = back[:, C:2 * C]
    filter_raw = back[:, 2 * C:]
    scale_factor = float(TOKENS) ** -0.5
    output = queries * conv
    filter_grad = filter_raw * scale_factor
    branch_grads = jnp.stack([cotangent * conv, grad_inner * value_rows, grad_inner * key_rows], axis=1).astype(jnp.bfloat16)
    summed = jax.ops.segment_sum(branch_grads.reshape(length, 3 * C).astype(jnp.float32), token_ids, num_segments=VOCAB)
    weight_grad = jnp.dot(embedding.astype(jnp.float32).T, summed, precision=lax.Precision.HIGHEST) * scale_factor
    return output, filter_grad, branch_grads, weight_grad.reshape(D, 3, N_RED, C // N_RED)
```

```python
import functools
import math

import jax
import jax.numpy as jnp
import numpy as np
from jax import lax
from jax.experimental import pallas as pl
from jax.experimental.pallas import tpu as pltpu
from jax.sharding import PartitionSpec as P

precise_mode = lax.Precision.HIGHEST
MESH = pl.DeviceIdType.MESH
VMEM = pl.BlockSpec(memory_space=pltpu.VMEM)
SHARES = (1,)
VMEM_BYTES = 67043328
NN = (((1,), (0,)), ((), ()))
NT = (((1,), (1,)), ((), ()))


def dot(left, right, dims=NN):
    return lax.dot_general(left, right, dims, preferred_element_type=jnp.float32)


def stack_split(value):
    high = value.astype(jnp.bfloat16).astype(jnp.float32)
    return jnp.concatenate([high, value - high], axis=0).astype(jnp.bfloat16)


def dot_split(value, matrix, dims=NN):
    both = dot(stack_split(value), matrix, dims)
    rows = value.shape[0]
    return both[:rows] + both[rows:]


def dot_both(value, matrix_high, matrix_low, dims=NN):
    high = value.astype(jnp.bfloat16)
    return dot_split(value, matrix_high, dims) + dot(high, matrix_low, dims)


def transform_tables(block, blocks):
    total = 2 * blocks * block
    place = np.arange(block)
    half = block // 2
    tables = np.zeros((2, 2 * block, 2 * block))
    even = 2 * np.pi * ((2 * blocks * place[:, None] * np.arange(half)[None, :]) % total) / total
    odd = 2 * np.pi * ((place[:, None] * (blocks + 2 * blocks * np.arange(half))[None, :]) % total) / total
    tables[0, :block, :half] = np.cos(even)
    tables[0, :block, block : block + half] = np.sin(even)
    tables[0, :block, block] = 1.0 - 2.0 * (place % 2)
    tables[0, block:, half:block] = np.cos(odd)
    tables[0, block:, block + half :] = np.sin(odd)
    psi = 2 * np.pi * ((place[:, None] * place[None, :]) % block) / block
    tables[1, :block, :block] = np.cos(psi)
    tables[1, :block, block:] = np.sin(psi)
    tables[1, block:, :block] = -np.sin(psi)
    tables[1, block:, block:] = np.cos(psi)
    tables = tables.astype(np.float32)
    high = tables.astype(jnp.bfloat16)
    low = (tables - high.astype(np.float32)).astype(jnp.bfloat16)
    alpha = 2 * np.pi * np.arange(blocks)[:, None] * place[None, :] / total
    return high, low, np.concatenate([np.cos(alpha), np.sin(alpha)]).astype(np.float32)


def phases(residue, blocks):
    if residue == 0:
        return [1.0] * blocks, [(-1.0) ** index for index in range(blocks)]
    turn = [math.pi * ((residue * index) % (2 * blocks)) / blocks for index in range(blocks)]
    return [math.cos(a) for a in turn], [math.sin(a) for a in turn]


def weighted(terms, weights):
    total = None
    for term, weight in zip(terms, weights):
        if abs(weight) < 1e-12:
            continue
        part = term if weight == 1.0 else (-term if weight == -1.0 else term * weight)
        total = part if total is None else total + part
    return total


def fold(pieces, residue, blocks):
    cosines, sines = phases(residue, blocks)
    return weighted(pieces, cosines), weighted(pieces, sines)


def combine(spectrum, block, sub, first):
    cos_part = spectrum[:, :block]
    sin_part = spectrum[:, block:]
    fc, ic, uc = (cos_part[at * sub : (at + 1) * sub] for at in range(3))
    fs, i_s, us = (sin_part[at * sub : (at + 1) * sub] for at in range(3))
    cc = [fc * ic, fc * uc, uc * ic]
    ss = [fs * i_s, fs * us, us * i_s]
    new_cos = [cc[0] - ss[0], cc[1] + ss[1], cc[2] + ss[2]]
    new_sin = [fc * i_s + fs * ic, fc * us - fs * uc, us * ic - uc * i_s]
    new_cos = jnp.concatenate(new_cos, axis=0)
    new_sin = jnp.concatenate(new_sin, axis=0)
    if first:
        lane = lax.broadcasted_iota(jnp.int32, new_cos.shape, 1) == 0
        new_cos = jnp.where(lane, 0.5 * jnp.concatenate(cc, axis=0), new_cos)
        new_sin = jnp.where(lane, 0.5 * jnp.concatenate(ss, axis=0), new_sin)
    return jnp.concatenate([new_cos, new_sin], axis=1)


def convolve(pieces, high_ref, low_ref, turn_ref, sub):
    blocks = len(pieces)
    block = pieces[0].shape[1]
    rows = 3 * sub
    scale = 1.0 / (blocks * block)
    turns = [(turn_ref[at : at + 1], turn_ref[blocks + at : blocks + at + 1]) for at in range(blocks)]
    first = dot_both(jnp.concatenate(fold(pieces, 0, blocks), axis=1), high_ref[0], low_ref[0])
    packed = []
    for residue in range(1, blocks):
        even, odd = fold(pieces, residue, blocks)
        cosine, sine = turns[residue]
        packed.append(
            jnp.concatenate([even * cosine - odd * sine, even * sine + odd * cosine], axis=1)
        )
    spectrum = dot_both(jnp.concatenate(packed, axis=0), high_ref[1], low_ref[1])
    joined = [
        combine(spectrum[at * rows : (at + 1) * rows], block, sub, False) * scale
        for at in range(blocks - 1)
    ]
    head = dot_both(combine(first, block, sub, True) * scale, high_ref[0], low_ref[0], NT)
    back = dot_both(jnp.concatenate(joined, axis=0), high_ref[1], low_ref[1], NT)
    cosines, sines = phases(0, blocks)
    results = [
        weighted([head[:, :block], head[:, block:]], [cosines[at], sines[at]])
        for at in range(blocks)
    ]
    for residue in range(1, blocks):
        real = back[(residue - 1) * rows : residue * rows, :block]
        imag = back[(residue - 1) * rows : residue * rows, block:]
        cosine, sine = turns[residue]
        cosines, sines = phases(residue, blocks)
        pair = [real * cosine + imag * sine, imag * cosine - real * sine]
        for at in range(blocks):
            results[at] = results[at] + weighted(pair, [cosines[at], sines[at]])
    return results


def greet(devices, count):
    me = lax.axis_index("seq")
    spot = lax.axis_index("red")
    barrier = pltpu.get_barrier_semaphore()
    for step in range(1, devices):
        peer = lax.rem(me + step, devices)
        pl.semaphore_signal(barrier, inc=1, device_id={"seq": peer}, device_id_type=MESH)

    @pl.when(spot > 0)
    def _():
        pl.semaphore_signal(barrier, inc=1, device_id={"red": spot - 1}, device_id_type=MESH)

    @pl.when(spot < count - 1)
    def _():
        pl.semaphore_signal(barrier, inc=1, device_id={"red": spot + 1}, device_id_type=MESH)


def meet(devices, count):
    spot = lax.axis_index("red")
    neighbours = jnp.where(spot > 0, 1, 0) + jnp.where(spot < count - 1, 1, 0)
    pl.semaphore_wait(pltpu.get_barrier_semaphore(), devices - 1 + neighbours)


def exchange(devices, source, target, send_sem, recv_sem, base):
    me = lax.axis_index("seq")
    copies = []
    for step in range(1, devices):
        peer = lax.rem(me + step, devices)
        copy = pltpu.make_async_remote_copy(
            src_ref=source(peer),
            dst_ref=target(me),
            send_sem=send_sem.at[base + step - 1],
            recv_sem=recv_sem.at[base + step - 1],
            device_id={"seq": peer},
            device_id_type=MESH,
        )
        copy.start()
        copies.append(copy)
    return copies


def chunk_sizes(piece):
    return [piece * share // sum(SHARES) for share in SHARES]


def main_kernel(
    devices, count, scale_factor,
    tok_hbm, emb_hbm, wt_hbm, filt_hbm, cot_hbm, high_hbm, low_hbm, turn_hbm,
    out_ref, fgrad_ref, grads_ref, weight_ref,
    tok_ref, emb_ref, wt_ref, filt_ref, cot_ref, high_ref, low_ref, turn_ref,
    part, from_left, from_right, all_ref, out_sig, sig, sending, recv, one_hot,
    load_sem, wt_sem, sig_send, sig_recv, res_send, res_recv,
    right_send, right_recv, left_send, left_recv,
    up_send, up_recv, down_send, down_recv,
):
    me = lax.axis_index("seq")
    spot = lax.axis_index("red")
    branches, _, piece, _ = wt_ref.shape
    tok_count, width = filt_ref.shape
    vocabulary = emb_ref.shape[0]
    sizes = chunk_sizes(piece)
    starts = [sum(sizes[:at]) for at in range(len(sizes))]
    chunks = len(sizes)
    last = count - 1
    greet(devices, count)

    def goal_at(index):
        return jnp.where(spot * 2 < count, last - index, index)

    def load(index, source, target):
        copy = pltpu.make_async_copy(source, target, load_sem.at[index])
        copy.start()
        return copy

    emb_load = load(0, emb_hbm, emb_ref)
    wt_loads = []
    for index in range(count):
        goal = goal_at(index)
        copy = pltpu.make_async_copy(wt_hbm.at[:, goal], wt_ref.at[:, goal], wt_sem.at[index])
        copy.start()
        wt_loads.append(copy)
    signal_loads = [
        load(1, filt_hbm, filt_ref), load(2, cot_hbm, cot_ref), load(3, tok_hbm, tok_ref),
    ]
    table_loads = [
        load(4, high_hbm, high_ref), load(5, low_hbm, low_ref), load(6, turn_hbm, turn_ref),
    ]
    above_spot = jnp.minimum(spot + 1, last)
    below_spot = jnp.maximum(spot - 1, 0)

    def view(ref, chunk, group):
        return ref.at[group, pl.ds(branches * starts[chunk], branches * sizes[chunk])]

    def hop(source, target, chunk, group, sends, recvs, neighbour):
        slot = chunk * count + group
        return pltpu.make_async_remote_copy(
            src_ref=view(source, chunk, group),
            dst_ref=view(target, chunk, group),
            send_sem=sends.at[slot],
            recv_sem=recvs.at[slot],
            device_id={"red": neighbour},
            device_id_type=MESH,
        )

    def right(chunk, group):
        return hop(part, from_left, chunk, group, right_send, right_recv, above_spot)

    def left(chunk, group):
        return hop(part, from_right, chunk, group, left_send, left_recv, below_spot)

    def up(chunk, group):
        return hop(all_ref, all_ref, chunk, group, up_send, up_recv, above_spot)

    def down(chunk, group):
        return hop(all_ref, all_ref, chunk, group, down_send, down_recv, below_spot)

    def add(target, source, chunk, group):
        view(target, chunk, group)[...] = view(target, chunk, group)[...] + view(source, chunk, group)[...]

    def products(index):
        goal = goal_at(index)
        wt_loads[index].wait()
        rows = jnp.concatenate([wt_ref[b, goal] for b in range(branches)], axis=0)
        product = dot(rows, emb_ref[...], NT)
        for start, size in zip(starts, sizes):
            for b in range(branches):
                base = branches * start + b * size
                part[goal, base : base + size] = product[b * piece + start : b * piece + start + size]

    def first_hop(chunk, index):
        @pl.when(spot == 0)
        def _():
            right(chunk, last - index).start()

        @pl.when(spot == last)
        def _():
            left(chunk, index).start()

    def middle_hops(chunk):
        for tick in range(1, last):
            goal = last - (tick - spot)

            @pl.when((spot > 0) & (tick >= spot) & (spot < goal))
            def _():
                right(chunk, goal).wait_recv()
                add(part, from_left, chunk, goal)
                right(chunk, goal).start()

            other = tick - (last - spot)

            @pl.when((spot < last) & (other >= 0) & (spot > other))
            def _():
                left(chunk, other).wait_recv()
                add(part, from_right, chunk, other)
                left(chunk, other).start()

    def arrive(chunk):
        @pl.when(spot > 0)
        def _():
            right(chunk, spot).wait_recv()
            add(part, from_left, chunk, spot)

        @pl.when(spot < last)
        def _():
            left(chunk, spot).wait_recv()
            add(part, from_right, chunk, spot)

        return view(part, chunk, spot)[...]

    def share(chunk):
        @pl.when(spot < last)
        def _():
            up(chunk, spot).start()

        @pl.when(spot > 0)
        def _():
            down(chunk, spot).start()

    def relay(chunk, sources, distance):
        for source in sources:
            if source < last:
                @pl.when((spot < last) & (spot - source == distance))
                def _():
                    up(chunk, source).wait_recv()
                    up(chunk, source).start()

            if source > 0:
                @pl.when((spot > 0) & (source - spot == distance))
                def _():
                    down(chunk, source).wait_recv()
                    down(chunk, source).start()

    inner = list(range(1, last))
    ends = [0, last]

    def relay_far(chunk):
        for distance in range(2, last):
            relay(chunk, range(count), distance)

    def collect(chunk):
        for step in range(1, count):
            @pl.when(spot == 0)
            def _():
                down(chunk, step).wait_recv()

            @pl.when(spot == last)
            def _():
                up(chunk, last - step).wait_recv()

    def weights(chunk):
        start, size = starts[chunk], sizes[chunk]
        blocks = jnp.concatenate([view(all_ref, chunk, group)[...] for group in range(count)], axis=0)
        product = dot_split(blocks, emb_ref[...]) * scale_factor
        for group in range(count):
            for b in range(branches):
                base = (group * branches + b) * size
                weight_ref[b, group, start : start + size] = product[base : base + size]

    def signal_rows(start, rows, at):
        return sig[at, start : start + rows]

    def channels(chunk, own):
        start, size = starts[chunk], sizes[chunk]
        projected = dot_split(own, one_hot[...])
        pieces = []
        held = []
        for at in range(devices):
            block = projected[:, at * tok_count : (at + 1) * tok_count]
            queries, key_rows, value_rows = (block[b * size : (b + 1) * size] for b in range(3))
            cotangent = signal_rows(piece + start, size, at)
            held.append((queries, key_rows, value_rows, cotangent))
            pieces.append(
                jnp.concatenate(
                    [signal_rows(start, size, at), key_rows * value_rows, cotangent * queries], axis=0
                )
            )
        results = convolve(pieces, high_ref, low_ref, turn_ref, size)
        rounded = []
        for at in range(devices):
            queries, key_rows, value_rows, cotangent = held[at]
            conv = results[at][:size]
            grad_inner = results[at][size : 2 * size]
            grads = jnp.concatenate(
                [cotangent * conv, grad_inner * value_rows, grad_inner * key_rows], axis=0
            ).astype(jnp.bfloat16)
            rounded.append(grads)
            base = 5 * start
            sending[at, base : base + size] = queries * conv
            sending[at, base + size : base + 2 * size] = results[at][2 * size :] * scale_factor
            sending[at, base + 2 * size : base + 5 * size] = grads.astype(jnp.float32)
        sums = dot(jnp.concatenate(rounded, axis=1), one_hot[...], NT)
        view(all_ref, chunk, spot)[...] = sums

    def positions(at):
        parts = [
            recv[peer, 5 * start + at * size : 5 * start + (at + 1) * size]
            for peer in range(devices)
            for start, size in zip(starts, sizes)
        ]
        return jnp.concatenate(parts, axis=0).T

    emb_load.wait()
    products(0)
    meet(devices, count)
    first_hop(0, 0)
    for copy in signal_loads:
        copy.wait()
    filt_t = filt_ref[...].T
    cot_t = cot_ref[...].T
    tok_rows = jnp.broadcast_to(tok_ref[...].astype(jnp.float32), (8, tok_count))
    for peer in range(devices):
        out_sig[peer, :piece] = filt_t[peer * piece : (peer + 1) * piece]
        out_sig[peer, piece : 2 * piece] = cot_t[peer * piece : (peer + 1) * piece]
        out_sig[peer, 2 * piece :] = tok_rows
    copies = exchange(devices, out_sig.at.__getitem__, sig.at.__getitem__, sig_send, sig_recv, 0)
    for index in range(1, count):
        products(index)
        if index < last:
            first_hop(0, index)
    for chunk in range(1, chunks):
        for index in range(last):
            first_hop(chunk, index)
    sig[me] = out_sig[me]
    sent = list(copies)
    arrivals = []
    for chunk in range(chunks):
        middle_hops(chunk)
        if chunk > 0:
            relay(chunk - 1, inner, 1)
        else:
            for copy in copies:
                copy.wait_recv()
            ids = jnp.concatenate([signal_rows(2 * piece, 1, at) for at in range(devices)], axis=1)
            vocab_rows = lax.broadcasted_iota(jnp.int32, (vocabulary, devices * tok_count), 0)
            one_hot[...] = jnp.where(vocab_rows == ids.astype(jnp.int32), 1.0, 0.0).astype(jnp.bfloat16)
            for copy in table_loads:
                copy.wait()
        channels(chunk, arrive(chunk))
        share(chunk)
        rows = pl.ds(5 * starts[chunk], 5 * sizes[chunk])
        more = exchange(
            devices,
            lambda peer, rows=rows: sending.at[peer, rows],
            lambda slot, rows=rows: recv.at[slot, rows],
            res_send, res_recv, chunk * (devices - 1),
        )
        recv[me, 5 * starts[chunk] : 5 * (starts[chunk] + sizes[chunk])] = sending[
            me, 5 * starts[chunk] : 5 * (starts[chunk] + sizes[chunk])
        ]
        sent += more
        arrivals += more
    final = chunks - 1
    for chunk in range(final):
        relay(chunk, ends, 1)
    relay(final, inner, 1)
    for chunk in range(final):
        relay_far(chunk)
    for chunk in range(final):
        collect(chunk)
        weights(chunk)
    relay(final, ends, 1)
    for copy in arrivals:
        copy.wait_recv()
    out_ref[...] = positions(0)
    fgrad_ref[...] = positions(1)
    for branch in range(branches):
        grads_ref[branch] = positions(2 + branch).astype(jnp.bfloat16)
    relay_far(final)
    collect(final)
    weights(final)
    for chunk in range(chunks):
        for group in range(count):
            @pl.when(spot < group)
            def _():
                right(chunk, group).wait_send()

            @pl.when(spot > group)
            def _():
                left(chunk, group).wait_send()

            @pl.when((spot >= group) & (spot < last))
            def _():
                up(chunk, group).wait_send()

            @pl.when((spot <= group) & (spot > 0))
            def _():
                down(chunk, group).wait_send()

    for copy in sent:
        copy.wait_send()


def final_kernel(out_in, fgrad_in, grads_in, weight_in, out_ref, fgrad_ref, grads_ref, weight_ref, sem):
    pairs = [(weight_in, weight_ref), (grads_in, grads_ref), (out_in, out_ref), (fgrad_in, fgrad_ref)]
    copies = [
        pltpu.make_async_copy(source, target, sem.at[index])
        for index, (source, target) in enumerate(pairs)
    ]
    for copy in copies:
        copy.start()
    for copy in copies:
        copy.wait()


def kernel_shards(devices, count, token_ids, embedding, proj_weight, filters, cotangent):
    tok_count, width = filters.shape
    vocabulary, depth = embedding.shape
    _, branches, _, piece = proj_weight.shape
    scale_factor = float(tok_count * devices) ** (-0.5)
    chunks = len(SHARES)
    f32 = jnp.float32
    bf16 = jnp.bfloat16
    dma = pltpu.SemaphoreType.DMA
    weight_t = jnp.transpose(proj_weight, (1, 2, 3, 0))
    high, low, turn = transform_tables(tok_count, devices)
    block = (count, branches * piece, vocabulary)
    message = (devices, 2 * piece + 8, tok_count)
    answer = (devices, 5 * piece, tok_count)
    results = (
        ((tok_count, width), f32),
        ((tok_count, width), f32),
        ((branches, tok_count, width), bf16),
        ((branches, count, piece, depth), f32),
    )
    kept = sum(math.prod(shape) * jnp.dtype(kind).itemsize for shape, kind in results) + 2**17
    held = pl.pallas_call(
        functools.partial(main_kernel, devices, count, scale_factor),
        out_shape=tuple(pltpu.VMEM(shape, kind) for shape, kind in results),
        in_specs=[pl.BlockSpec(memory_space=pltpu.HBM)] * 8,
        out_specs=(VMEM,) * 4,
        scratch_shapes=[
            pltpu.VMEM((1, tok_count), jnp.int32),
            pltpu.VMEM(embedding.shape, bf16),
            pltpu.VMEM(weight_t.shape, bf16),
            pltpu.VMEM(filters.shape, f32),
            pltpu.VMEM(cotangent.shape, f32),
            pltpu.VMEM(high.shape, bf16),
            pltpu.VMEM(low.shape, bf16),
            pltpu.VMEM(turn.shape, f32),
            pltpu.VMEM(block, f32),
            pltpu.VMEM(block, f32),
            pltpu.VMEM(block, f32),
            pltpu.VMEM(block, f32),
            pltpu.VMEM(message, f32),
            pltpu.VMEM(message, f32),
            pltpu.VMEM(answer, f32),
            pltpu.VMEM(answer, f32),
            pltpu.VMEM((vocabulary, devices * tok_count), bf16),
            dma((7,)),
            dma((count,)),
            dma((devices - 1,)),
            dma((devices - 1,)),
            dma((chunks * (devices - 1),)),
            dma((chunks * (devices - 1),)),
        ]
        + [dma((chunks * count,))] * 8,
        compiler_params=pltpu.CompilerParams(
            collective_id=0, has_side_effects=True, vmem_limit_bytes=VMEM_BYTES - kept
        ),
        name="hyena_exchange",
    )(
        token_ids.reshape(1, tok_count), embedding, weight_t, filters, cotangent,
        jnp.asarray(high), jnp.asarray(low), jnp.asarray(turn),
    )
    output, filter_grad, grads, weight = pl.pallas_call(
        final_kernel,
        out_shape=tuple(jax.ShapeDtypeStruct(shape, kind) for shape, kind in results),
        in_specs=[VMEM] * 4,
        out_specs=(pl.BlockSpec(memory_space=pltpu.HBM),) * 4,
        scratch_shapes=[dma((4,))],
        compiler_params=pltpu.CompilerParams(vmem_limit_bytes=2**20),
        name="finish",
    )(*held)
    return (
        output,
        filter_grad,
        jnp.transpose(grads, (1, 0, 2)),
        jnp.transpose(weight, (3, 0, 1, 2)),
    )


def fits_kernels(devices, count, token_ids, embedding, proj_weight, filters):
    tok_count, width = filters.shape
    vocabulary, depth = embedding.shape
    _, branches, red_count, piece = proj_weight.shape
    lanes = (tok_count, vocabulary, depth)
    aligned = all(size % 128 == 0 for size in lanes) and piece % (8 * sum(SHARES)) == 0
    one_hot = vocabulary * tok_count * devices * 8
    held = 4 * branches * piece * (4 * count * vocabulary + 2 * count * depth)
    sides = 4 * tok_count * devices * 20 * piece + 16 * vocabulary * depth
    return (
        aligned
        and count > 1
        and branches == 3
        and red_count == count
        and width == devices * piece
        and one_hot + held + sides < 36 * 2**20
    )


def angles(numbers, modulus, direction):
    phase = (numbers % modulus).astype(jnp.float32) * (direction * 2.0 * math.pi / modulus)
    return (jnp.cos(phase), jnp.sin(phase))


def rotate(real_part, imag_part, cosine, sine_part):
    return (real_part * cosine - imag_part * sine_part, real_part * sine_part + imag_part * cosine)


def complex_einsum(formula, matrix, values):
    mat_real, mat_imag = matrix
    val_real, val_imag = values
    real_out = jnp.einsum(formula, mat_real, val_real, precision=precise_mode) - jnp.einsum(
        formula, mat_imag, val_imag, precision=precise_mode
    )
    imag_out = jnp.einsum(formula, mat_real, val_imag, precision=precise_mode) + jnp.einsum(
        formula, mat_imag, val_real, precision=precise_mode
    )
    return (real_out, imag_out)


def factors(length_total):
    first_factor = 1
    for candidate in range(1, math.isqrt(length_total) + 1):
        if length_total % candidate == 0:
            first_factor = candidate
    return (first_factor, length_total // first_factor)


def combine_spectra(spec_real, spec_imag, width):
    filt_re = spec_real[..., :width]
    inner_re = spec_real[..., width : 2 * width]
    up_re = spec_real[..., 2 * width :]
    filt_im = spec_imag[..., :width]
    inner_im = spec_imag[..., width : 2 * width]
    up_im = spec_imag[..., 2 * width :]
    joined_real = jnp.concatenate(
        [
            filt_re * inner_re - filt_im * inner_im,
            filt_re * up_re + filt_im * up_im,
            up_re * inner_re + up_im * inner_im,
        ],
        axis=-1,
    )
    joined_imag = jnp.concatenate(
        [
            filt_re * inner_im + filt_im * inner_re,
            filt_re * up_im - filt_im * up_re,
            up_im * inner_re - up_re * inner_im,
        ],
        axis=-1,
    )
    return (joined_real, joined_imag)


def local_convolve(signals):
    length, branch_count, narrow = signals.shape
    total = 2 * length
    first_factor, second_factor = factors(total)
    flat = signals.reshape(length, branch_count * narrow)
    padded = jnp.concatenate([flat, jnp.zeros_like(flat)], axis=0).reshape(
        first_factor, second_factor, branch_count * narrow
    )
    first_index = jnp.arange(first_factor, dtype=jnp.int32)
    second_index = jnp.arange(second_factor, dtype=jnp.int32)
    cosine, sine_part = angles(first_index[:, None] * first_index[None, :], first_factor, -1.0)
    real_part = jnp.einsum("kn,nbm->kbm", cosine, padded, precision=precise_mode)
    imag_part = jnp.einsum("kn,nbm->kbm", sine_part, padded, precision=precise_mode)
    cosine, sine_part = angles(first_index[:, None] * second_index[None, :], total, -1.0)
    real_part, imag_part = rotate(real_part, imag_part, cosine[:, :, None], sine_part[:, :, None])
    real_part, imag_part = complex_einsum(
        "lb,kbm->klm",
        angles(second_index[:, None] * second_index[None, :], second_factor, -1.0),
        (real_part, imag_part),
    )
    real_part, imag_part = combine_spectra(real_part, imag_part, narrow)
    real_part, imag_part = complex_einsum(
        "bl,klm->kbm",
        angles(second_index[:, None] * second_index[None, :], second_factor, 1.0),
        (real_part, imag_part),
    )
    cosine, sine_part = angles(first_index[:, None] * second_index[None, :], total, 1.0)
    real_part, imag_part = rotate(real_part, imag_part, cosine[:, :, None], sine_part[:, :, None])
    cosine, sine_part = angles(first_index[:, None] * first_index[None, :], first_factor, 1.0)
    result = jnp.einsum("nk,kbm->nbm", cosine, real_part, precision=precise_mode) - jnp.einsum(
        "nk,kbm->nbm", sine_part, imag_part, precision=precise_mode
    )
    result = result.reshape(total, branch_count * narrow)[:length] / total
    return result.reshape(length, branch_count, narrow)


def shards(token_ids, embedding, proj_weight, filters, cotangent):
    tok_count = token_ids.shape[0]
    devices = lax.axis_size("seq")
    count = lax.axis_size("red")
    if fits_kernels(devices, count, token_ids, embedding, proj_weight, filters):
        return kernel_shards(
            devices, count, token_ids, embedding, proj_weight, filters, cotangent
        )
    width = filters.shape[1]
    vocabulary = embedding.shape[0]
    width_rows, branches, red_count, piece = proj_weight.shape
    scale_factor = float(tok_count * devices) ** (-0.5)
    table = jnp.dot(
        embedding,
        proj_weight.reshape(width_rows, branches * red_count * piece),
        preferred_element_type=jnp.float32,
    )
    table = table.reshape(vocabulary, branches, red_count, piece)
    own_table = lax.psum_scatter(table, "red", scatter_dimension=2, tiled=True)
    full_table = lax.all_gather(own_table, "seq", axis=3, tiled=True)
    projected = jnp.take(full_table, token_ids, axis=0)
    projected = projected.reshape(tok_count, branches, width)
    queries = projected[:, 0]
    key_rows = projected[:, 1]
    value_rows = projected[:, 2]
    inner = key_rows * value_rows
    upstream = cotangent * queries
    stacked = jnp.stack([filters, inner, upstream], axis=1)
    whole_length = lax.all_to_all(stacked, "seq", split_axis=2, concat_axis=0, tiled=True)
    results = local_convolve(whole_length)
    returned = lax.all_to_all(results, "seq", split_axis=0, concat_axis=2, tiled=True)
    conv = returned[:, 0]
    grad_inner = returned[:, 1]
    filter_raw = returned[:, 2]
    output = queries * conv
    filter_grad = filter_raw * scale_factor
    branch_grads = jnp.stack(
        [cotangent * conv, grad_inner * value_rows, grad_inner * key_rows], axis=1
    ).astype(jnp.bfloat16)
    one_hot = (token_ids[:, None] == lax.iota(jnp.int32, vocabulary)[None, :]).astype(jnp.bfloat16)
    token_sums = lax.dot_general(
        one_hot,
        branch_grads.reshape(tok_count, branches * width),
        (((0,), (0,)), ((), ())),
        preferred_element_type=jnp.float32,
    )
    summed = lax.psum_scatter(
        token_sums.reshape(vocabulary, branches, width), "seq", scatter_dimension=2, tiled=True
    )
    gathered = lax.all_gather(summed[:, :, None, :], "red", axis=2, tiled=True)
    weight_grad = (
        lax.dot_general(
            embedding.astype(jnp.float32),
            gathered.reshape(vocabulary, branches * red_count * piece),
            (((0,), (0,)), ((), ())),
            precision=precise_mode,
        )
        * scale_factor
    )
    return (
        output,
        filter_grad,
        branch_grads,
        weight_grad.reshape(width_rows, branches, red_count, piece),
    )


def solution(mesh):
    in_specs = (
        P("seq"),
        P(None, "red"),
        P("red", None, None, "seq"),
        P("seq", "red"),
        P("seq", "red"),
    )
    out_specs = (
        P("seq", "red"),
        P("seq", "red"),
        P("seq", None, "red"),
        P("red", None, None, "seq"),
    )
    return jax.shard_map(shards, mesh=mesh, in_specs=in_specs, out_specs=out_specs, check_vma=False)
```

```python
import functools
import math

import jax
import jax.numpy as jnp
import numpy as np
from jax import lax
from jax.experimental import pallas as pl
from jax.experimental.pallas import tpu as pltpu
from jax.sharding import PartitionSpec as P

precise_mode = lax.Precision.HIGHEST
MESH = pl.DeviceIdType.MESH
VMEM = pl.BlockSpec(memory_space=pltpu.VMEM)
SHARES = (1,)
PIECES = 4
VMEM_BYTES = 67043328
NN = (((1,), (0,)), ((), ()))
NT = (((1,), (1,)), ((), ()))


def dot(left, right, dims=NN):
    return lax.dot_general(left, right, dims, preferred_element_type=jnp.float32)


def stack_split(value):
    high = value.astype(jnp.bfloat16).astype(jnp.float32)
    return jnp.concatenate([high, value - high], axis=0).astype(jnp.bfloat16)


def dot_split(value, matrix, dims=NN):
    both = dot(stack_split(value), matrix, dims)
    rows = value.shape[0]
    return both[:rows] + both[rows:]


def dot_both(value, matrix_high, matrix_low, dims=NN):
    high = value.astype(jnp.bfloat16)
    return dot_split(value, matrix_high, dims) + dot(high, matrix_low, dims)


def transform_tables(block, blocks):
    total = 2 * blocks * block
    place = np.arange(block)
    half = block // 2
    tables = np.zeros((2, 2 * block, 2 * block))
    even = 2 * np.pi * ((2 * blocks * place[:, None] * np.arange(half)[None, :]) % total) / total
    odd = 2 * np.pi * ((place[:, None] * (blocks + 2 * blocks * np.arange(half))[None, :]) % total) / total
    tables[0, :block, :half] = np.cos(even)
    tables[0, :block, block : block + half] = np.sin(even)
    tables[0, :block, block] = 1.0 - 2.0 * (place % 2)
    tables[0, block:, half:block] = np.cos(odd)
    tables[0, block:, block + half :] = np.sin(odd)
    psi = 2 * np.pi * ((place[:, None] * place[None, :]) % block) / block
    tables[1, :block, :block] = np.cos(psi)
    tables[1, :block, block:] = np.sin(psi)
    tables[1, block:, :block] = -np.sin(psi)
    tables[1, block:, block:] = np.cos(psi)
    tables = tables.astype(np.float32)
    high = tables.astype(jnp.bfloat16)
    low = (tables - high.astype(np.float32)).astype(jnp.bfloat16)
    alpha = 2 * np.pi * np.arange(blocks)[:, None] * place[None, :] / total
    return high, low, np.concatenate([np.cos(alpha), np.sin(alpha)]).astype(np.float32)


def phases(residue, blocks):
    if residue == 0:
        return [1.0] * blocks, [(-1.0) ** index for index in range(blocks)]
    turn = [math.pi * ((residue * index) % (2 * blocks)) / blocks for index in range(blocks)]
    return [math.cos(a) for a in turn], [math.sin(a) for a in turn]


def weighted(terms, weights):
    total = None
    for term, weight in zip(terms, weights):
        if abs(weight) < 1e-12:
            continue
        part = term if weight == 1.0 else (-term if weight == -1.0 else term * weight)
        total = part if total is None else total + part
    return total


def fold(pieces, residue, blocks):
    cosines, sines = phases(residue, blocks)
    return weighted(pieces, cosines), weighted(pieces, sines)


def combine(spectrum, block, sub, first):
    cos_part = spectrum[:, :block]
    sin_part = spectrum[:, block:]
    fc, ic, uc = (cos_part[at * sub : (at + 1) * sub] for at in range(3))
    fs, i_s, us = (sin_part[at * sub : (at + 1) * sub] for at in range(3))
    cc = [fc * ic, fc * uc, uc * ic]
    ss = [fs * i_s, fs * us, us * i_s]
    new_cos = [cc[0] - ss[0], cc[1] + ss[1], cc[2] + ss[2]]
    new_sin = [fc * i_s + fs * ic, fc * us - fs * uc, us * ic - uc * i_s]
    new_cos = jnp.concatenate(new_cos, axis=0)
    new_sin = jnp.concatenate(new_sin, axis=0)
    if first:
        lane = lax.broadcasted_iota(jnp.int32, new_cos.shape, 1) == 0
        new_cos = jnp.where(lane, 0.5 * jnp.concatenate(cc, axis=0), new_cos)
        new_sin = jnp.where(lane, 0.5 * jnp.concatenate(ss, axis=0), new_sin)
    return jnp.concatenate([new_cos, new_sin], axis=1)


def convolve(pieces, high_ref, low_ref, turn_ref, sub):
    blocks = len(pieces)
    block = pieces[0].shape[1]
    rows = 3 * sub
    scale = 1.0 / (blocks * block)
    turns = [(turn_ref[at : at + 1], turn_ref[blocks + at : blocks + at + 1]) for at in range(blocks)]
    first = dot_both(jnp.concatenate(fold(pieces, 0, blocks), axis=1), high_ref[0], low_ref[0])
    packed = []
    for residue in range(1, blocks):
        even, odd = fold(pieces, residue, blocks)
        cosine, sine = turns[residue]
        packed.append(
            jnp.concatenate([even * cosine - odd * sine, even * sine + odd * cosine], axis=1)
        )
    spectrum = dot_both(jnp.concatenate(packed, axis=0), high_ref[1], low_ref[1])
    joined = [
        combine(spectrum[at * rows : (at + 1) * rows], block, sub, False) * scale
        for at in range(blocks - 1)
    ]
    head = dot_both(combine(first, block, sub, True) * scale, high_ref[0], low_ref[0], NT)
    back = dot_both(jnp.concatenate(joined, axis=0), high_ref[1], low_ref[1], NT)
    cosines, sines = phases(0, blocks)
    results = [
        weighted([head[:, :block], head[:, block:]], [cosines[at], sines[at]])
        for at in range(blocks)
    ]
    for residue in range(1, blocks):
        real = back[(residue - 1) * rows : residue * rows, :block]
        imag = back[(residue - 1) * rows : residue * rows, block:]
        cosine, sine = turns[residue]
        cosines, sines = phases(residue, blocks)
        pair = [real * cosine + imag * sine, imag * cosine - real * sine]
        for at in range(blocks):
            results[at] = results[at] + weighted(pair, [cosines[at], sines[at]])
    return results


def greet(devices, count):
    me = lax.axis_index("seq")
    spot = lax.axis_index("red")
    barrier = pltpu.get_barrier_semaphore()
    for step in range(1, devices):
        peer = lax.rem(me + step, devices)
        pl.semaphore_signal(barrier, inc=1, device_id={"seq": peer}, device_id_type=MESH)

    @pl.when(spot > 0)
    def _():
        pl.semaphore_signal(barrier, inc=1, device_id={"red": spot - 1}, device_id_type=MESH)

    @pl.when(spot < count - 1)
    def _():
        pl.semaphore_signal(barrier, inc=1, device_id={"red": spot + 1}, device_id_type=MESH)


def meet(devices, count):
    spot = lax.axis_index("red")
    neighbours = jnp.where(spot > 0, 1, 0) + jnp.where(spot < count - 1, 1, 0)
    pl.semaphore_wait(pltpu.get_barrier_semaphore(), devices - 1 + neighbours)


def exchange(devices, source, target, send_sem, recv_sem, base):
    me = lax.axis_index("seq")
    copies = []
    for step in range(1, devices):
        peer = lax.rem(me + step, devices)
        copy = pltpu.make_async_remote_copy(
            src_ref=source(peer),
            dst_ref=target(me),
            send_sem=send_sem.at[base + step - 1],
            recv_sem=recv_sem.at[base + step - 1],
            device_id={"seq": peer},
            device_id_type=MESH,
        )
        copy.start()
        copies.append(copy)
    return copies


def chunk_sizes(piece):
    return [piece * share // sum(SHARES) for share in SHARES]


def main_kernel(
    devices, count, scale_factor,
    tok_hbm, emb_hbm, wt_hbm, filt_hbm, cot_hbm, high_hbm, low_hbm, turn_hbm,
    out_ref, fgrad_ref, grads_ref, weight_ref,
    tok_ref, emb_ref, wt_ref, filt_ref, cot_ref, high_ref, low_ref, turn_ref,
    part, from_left, from_right, all_ref, out_sig, sig, sending, recv, one_hot,
    load_sem, wt_sem, sig_send, sig_recv, res_send, res_recv,
    right_send, right_recv, left_send, left_recv,
    up_send, up_recv, down_send, down_recv,
):
    me = lax.axis_index("seq")
    spot = lax.axis_index("red")
    branches, _, piece, _ = wt_ref.shape
    tok_count, width = filt_ref.shape
    vocabulary = emb_ref.shape[0]
    sizes = chunk_sizes(piece)
    starts = [sum(sizes[:at]) for at in range(len(sizes))]
    chunks = len(sizes)
    last = count - 1
    greet(devices, count)

    def goal_at(index):
        return jnp.where(spot * 2 < count, last - index, index)

    def load(index, source, target):
        copy = pltpu.make_async_copy(source, target, load_sem.at[index])
        copy.start()
        return copy

    emb_load = load(0, emb_hbm, emb_ref)
    wt_loads = []
    for index in range(count):
        goal = goal_at(index)
        copy = pltpu.make_async_copy(wt_hbm.at[:, goal], wt_ref.at[:, goal], wt_sem.at[index])
        copy.start()
        wt_loads.append(copy)
    signal_loads = [
        load(1, filt_hbm, filt_ref), load(2, cot_hbm, cot_ref), load(3, tok_hbm, tok_ref),
    ]
    table_loads = [
        load(4, high_hbm, high_ref), load(5, low_hbm, low_ref), load(6, turn_hbm, turn_ref),
    ]
    above_spot = jnp.minimum(spot + 1, last)
    below_spot = jnp.maximum(spot - 1, 0)

    def view(ref, chunk, group, at=None):
        rows = branches * sizes[chunk]
        base = branches * starts[chunk]
        if at is not None:
            rows //= PIECES
            base += at * rows
        return ref.at[group, pl.ds(base, rows)]

    def hop(source, target, chunk, group, at, sends, recvs, neighbour):
        slot = (chunk * count + group) * PIECES + at
        return pltpu.make_async_remote_copy(
            src_ref=view(source, chunk, group, at),
            dst_ref=view(target, chunk, group, at),
            send_sem=sends.at[slot],
            recv_sem=recvs.at[slot],
            device_id={"red": neighbour},
            device_id_type=MESH,
        )

    def right(chunk, group, at):
        return hop(part, from_left, chunk, group, at, right_send, right_recv, above_spot)

    def left(chunk, group, at):
        return hop(part, from_right, chunk, group, at, left_send, left_recv, below_spot)

    def up(chunk, group, at):
        return hop(all_ref, all_ref, chunk, group, at, up_send, up_recv, above_spot)

    def down(chunk, group, at):
        return hop(all_ref, all_ref, chunk, group, at, down_send, down_recv, below_spot)

    def add(target, source, chunk, group, at):
        piece_ref = view(target, chunk, group, at)
        piece_ref[...] = piece_ref[...] + view(source, chunk, group, at)[...]

    def products(index):
        goal = goal_at(index)
        wt_loads[index].wait()
        rows = jnp.concatenate([wt_ref[b, goal] for b in range(branches)], axis=0)
        product = dot(rows, emb_ref[...], NT)
        for start, size in zip(starts, sizes):
            for b in range(branches):
                base = branches * start + b * size
                part[goal, base : base + size] = product[b * piece + start : b * piece + start + size]

    def first_hop(chunk, index):
        @pl.when(spot == 0)
        def _():
            for at in range(PIECES):
                right(chunk, last - index, at).start()

        @pl.when(spot == last)
        def _():
            for at in range(PIECES):
                left(chunk, index, at).start()

    def middle_hops(chunk):
        for tick in range(1, last):
            for at in range(PIECES):
                goal = last - (tick - spot)

                @pl.when((spot > 0) & (tick >= spot) & (spot < goal))
                def _():
                    right(chunk, goal, at).wait_recv()
                    add(part, from_left, chunk, goal, at)
                    right(chunk, goal, at).start()

                other = tick - (last - spot)

                @pl.when((spot < last) & (other >= 0) & (spot > other))
                def _():
                    left(chunk, other, at).wait_recv()
                    add(part, from_right, chunk, other, at)
                    left(chunk, other, at).start()

    def arrive(chunk):
        for at in range(PIECES):
            @pl.when(spot > 0)
            def _():
                right(chunk, spot, at).wait_recv()
                add(part, from_left, chunk, spot, at)

            @pl.when(spot < last)
            def _():
                left(chunk, spot, at).wait_recv()
                add(part, from_right, chunk, spot, at)

        return view(part, chunk, spot)[...]

    def share(chunk):
        for at in range(PIECES):
            @pl.when(spot < last)
            def _():
                up(chunk, spot, at).start()

            @pl.when(spot > 0)
            def _():
                down(chunk, spot, at).start()

    def relay(chunk, step):
        below = spot - step
        above = spot + step
        for at in range(PIECES):
            @pl.when((below >= 0) & (spot < last))
            def _():
                up(chunk, below, at).wait_recv()
                up(chunk, below, at).start()

            @pl.when((above < count) & (spot > 0))
            def _():
                down(chunk, above, at).wait_recv()
                down(chunk, above, at).start()

    def nearest(step):
        group = 0
        for place in range(count):
            order = sorted(range(count), key=lambda other: (abs(other - place), abs(2 * other - last)))
            group = jnp.where(spot == place, order[step], group)
        return group

    def collect(chunk, step):
        for at in range(PIECES):
            @pl.when(spot == 0)
            def _():
                down(chunk, step, at).wait_recv()

            @pl.when(spot == last)
            def _():
                up(chunk, last - step, at).wait_recv()

    def weights(chunk, step):
        start, size = starts[chunk], sizes[chunk]
        group = nearest(step)
        product = dot_split(view(all_ref, chunk, group)[...], emb_ref[...]) * scale_factor
        for b in range(branches):
            weight_ref[b, group, start : start + size] = product[b * size : (b + 1) * size]

    def signal_rows(start, rows, at):
        return sig[at, start : start + rows]

    def channels(chunk, own):
        start, size = starts[chunk], sizes[chunk]
        projected = dot_split(own, one_hot[...])
        pieces = []
        held = []
        for at in range(devices):
            block = projected[:, at * tok_count : (at + 1) * tok_count]
            queries, key_rows, value_rows = (block[b * size : (b + 1) * size] for b in range(3))
            cotangent = signal_rows(piece + start, size, at)
            held.append((queries, key_rows, value_rows, cotangent))
            pieces.append(
                jnp.concatenate(
                    [signal_rows(start, size, at), key_rows * value_rows, cotangent * queries], axis=0
                )
            )
        results = convolve(pieces, high_ref, low_ref, turn_ref, size)
        rounded = []
        for at in range(devices):
            queries, key_rows, value_rows, cotangent = held[at]
            conv = results[at][:size]
            grad_inner = results[at][size : 2 * size]
            grads = jnp.concatenate(
                [cotangent * conv, grad_inner * value_rows, grad_inner * key_rows], axis=0
            ).astype(jnp.bfloat16)
            rounded.append(grads)
            base = 5 * start
            sending[at, base : base + size] = queries * conv
            sending[at, base + size : base + 2 * size] = results[at][2 * size :] * scale_factor
            sending[at, base + 2 * size : base + 5 * size] = grads.astype(jnp.float32)
        sums = dot(jnp.concatenate(rounded, axis=1), one_hot[...], NT)
        view(all_ref, chunk, spot)[...] = sums

    def positions(at):
        parts = [
            recv[peer, 5 * start + at * size : 5 * start + (at + 1) * size]
            for peer in range(devices)
            for start, size in zip(starts, sizes)
        ]
        return jnp.concatenate(parts, axis=0).T

    emb_load.wait()
    products(0)
    meet(devices, count)
    first_hop(0, 0)
    for copy in signal_loads:
        copy.wait()
    filt_t = filt_ref[...].T
    cot_t = cot_ref[...].T
    tok_rows = jnp.broadcast_to(tok_ref[...].astype(jnp.float32), (8, tok_count))
    for peer in range(devices):
        out_sig[peer, :piece] = filt_t[peer * piece : (peer + 1) * piece]
        out_sig[peer, piece : 2 * piece] = cot_t[peer * piece : (peer + 1) * piece]
        out_sig[peer, 2 * piece :] = tok_rows
    copies = exchange(devices, out_sig.at.__getitem__, sig.at.__getitem__, sig_send, sig_recv, 0)
    for index in range(1, count):
        products(index)
        if index < last:
            first_hop(0, index)
    for chunk in range(1, chunks):
        for index in range(last):
            first_hop(chunk, index)
    sig[me] = out_sig[me]
    sent = list(copies)
    arrivals = []
    for chunk in range(chunks):
        middle_hops(chunk)
        if chunk == 0:
            for copy in copies:
                copy.wait_recv()
            ids = jnp.concatenate([signal_rows(2 * piece, 1, at) for at in range(devices)], axis=1)
            vocab_rows = lax.broadcasted_iota(jnp.int32, (vocabulary, devices * tok_count), 0)
            one_hot[...] = jnp.where(vocab_rows == ids.astype(jnp.int32), 1.0, 0.0).astype(jnp.bfloat16)
            for copy in table_loads:
                copy.wait()
        channels(chunk, arrive(chunk))
        share(chunk)
        rows = pl.ds(5 * starts[chunk], 5 * sizes[chunk])
        more = exchange(
            devices,
            lambda peer, rows=rows: sending.at[peer, rows],
            lambda slot, rows=rows: recv.at[slot, rows],
            res_send, res_recv, chunk * (devices - 1),
        )
        recv[me, 5 * starts[chunk] : 5 * (starts[chunk] + sizes[chunk])] = sending[
            me, 5 * starts[chunk] : 5 * (starts[chunk] + sizes[chunk])
        ]
        sent += more
        arrivals += more
        weights(chunk, 0)
    for chunk in range(chunks):
        for step in range(1, last):
            relay(chunk, step)
    for step in range(1, count):
        for chunk in range(chunks):
            if step == last and chunk == chunks - 1:
                for copy in arrivals:
                    copy.wait_recv()
                out_ref[...] = positions(0)
                fgrad_ref[...] = positions(1)
                for branch in range(branches):
                    grads_ref[branch] = positions(2 + branch).astype(jnp.bfloat16)
            collect(chunk, step)
            weights(chunk, step)
    for chunk in range(chunks):
        for group in range(count):
            for at in range(PIECES):
                @pl.when(spot < group)
                def _():
                    right(chunk, group, at).wait_send()

                @pl.when(spot > group)
                def _():
                    left(chunk, group, at).wait_send()

                @pl.when((spot >= group) & (spot < last))
                def _():
                    up(chunk, group, at).wait_send()

                @pl.when((spot <= group) & (spot > 0))
                def _():
                    down(chunk, group, at).wait_send()

    for copy in sent:
        copy.wait_send()


def final_kernel(out_in, fgrad_in, grads_in, weight_in, out_ref, fgrad_ref, grads_ref, weight_ref, sem):
    pairs = [(weight_in, weight_ref), (grads_in, grads_ref), (out_in, out_ref), (fgrad_in, fgrad_ref)]
    copies = [
        pltpu.make_async_copy(source, target, sem.at[index])
        for index, (source, target) in enumerate(pairs)
    ]
    for copy in copies:
        copy.start()
    for copy in copies:
        copy.wait()


def kernel_shards(devices, count, token_ids, embedding, proj_weight, filters, cotangent):
    tok_count, width = filters.shape
    vocabulary, depth = embedding.shape
    _, branches, _, piece = proj_weight.shape
    scale_factor = float(tok_count * devices) ** (-0.5)
    chunks = len(SHARES)
    f32 = jnp.float32
    bf16 = jnp.bfloat16
    dma = pltpu.SemaphoreType.DMA
    weight_t = jnp.transpose(proj_weight, (1, 2, 3, 0))
    high, low, turn = transform_tables(tok_count, devices)
    block = (count, branches * piece, vocabulary)
    message = (devices, 2 * piece + 8, tok_count)
    answer = (devices, 5 * piece, tok_count)
    results = (
        ((tok_count, width), f32),
        ((tok_count, width), f32),
        ((branches, tok_count, width), bf16),
        ((branches, count, piece, depth), f32),
    )
    kept = sum(math.prod(shape) * jnp.dtype(kind).itemsize for shape, kind in results) + 2**17
    held = pl.pallas_call(
        functools.partial(main_kernel, devices, count, scale_factor),
        out_shape=tuple(pltpu.VMEM(shape, kind) for shape, kind in results),
        in_specs=[pl.BlockSpec(memory_space=pltpu.HBM)] * 8,
        out_specs=(VMEM,) * 4,
        scratch_shapes=[
            pltpu.VMEM((1, tok_count), jnp.int32),
            pltpu.VMEM(embedding.shape, bf16),
            pltpu.VMEM(weight_t.shape, bf16),
            pltpu.VMEM(filters.shape, f32),
            pltpu.VMEM(cotangent.shape, f32),
            pltpu.VMEM(high.shape, bf16),
            pltpu.VMEM(low.shape, bf16),
            pltpu.VMEM(turn.shape, f32),
            pltpu.VMEM(block, f32),
            pltpu.VMEM(block, f32),
            pltpu.VMEM(block, f32),
            pltpu.VMEM(block, f32),
            pltpu.VMEM(message, f32),
            pltpu.VMEM(message, f32),
            pltpu.VMEM(answer, f32),
            pltpu.VMEM(answer, f32),
            pltpu.VMEM((vocabulary, devices * tok_count), bf16),
            dma((7,)),
            dma((count,)),
            dma((devices - 1,)),
            dma((devices - 1,)),
            dma((chunks * (devices - 1),)),
            dma((chunks * (devices - 1),)),
        ]
        + [dma((chunks * count * PIECES,))] * 8,
        compiler_params=pltpu.CompilerParams(
            collective_id=0, has_side_effects=True, vmem_limit_bytes=VMEM_BYTES - kept
        ),
        name="hyena_exchange",
    )(
        token_ids.reshape(1, tok_count), embedding, weight_t, filters, cotangent,
        jnp.asarray(high), jnp.asarray(low), jnp.asarray(turn),
    )
    output, filter_grad, grads, weight = pl.pallas_call(
        final_kernel,
        out_shape=tuple(jax.ShapeDtypeStruct(shape, kind) for shape, kind in results),
        in_specs=[VMEM] * 4,
        out_specs=(pl.BlockSpec(memory_space=pltpu.HBM),) * 4,
        scratch_shapes=[dma((4,))],
        compiler_params=pltpu.CompilerParams(vmem_limit_bytes=2**20),
        name="finish",
    )(*held)
    return (
        output,
        filter_grad,
        jnp.transpose(grads, (1, 0, 2)),
        jnp.transpose(weight, (3, 0, 1, 2)),
    )


def fits_kernels(devices, count, token_ids, embedding, proj_weight, filters):
    tok_count, width = filters.shape
    vocabulary, depth = embedding.shape
    _, branches, red_count, piece = proj_weight.shape
    lanes = (tok_count, vocabulary, depth)
    aligned = all(size % 128 == 0 for size in lanes) and piece % (8 * sum(SHARES)) == 0 and branches * piece % (8 * sum(SHARES) * PIECES) == 0
    one_hot = vocabulary * tok_count * devices * 8
    held = 4 * branches * piece * (4 * count * vocabulary + 2 * count * depth)
    sides = 4 * tok_count * devices * 20 * piece + 16 * vocabulary * depth
    return (
        aligned
        and count > 1
        and branches == 3
        and red_count == count
        and width == devices * piece
        and one_hot + held + sides < 36 * 2**20
    )


def angles(numbers, modulus, direction):
    phase = (numbers % modulus).astype(jnp.float32) * (direction * 2.0 * math.pi / modulus)
    return (jnp.cos(phase), jnp.sin(phase))


def rotate(real_part, imag_part, cosine, sine_part):
    return (real_part * cosine - imag_part * sine_part, real_part * sine_part + imag_part * cosine)


def complex_einsum(formula, matrix, values):
    mat_real, mat_imag = matrix
    val_real, val_imag = values
    real_out = jnp.einsum(formula, mat_real, val_real, precision=precise_mode) - jnp.einsum(
        formula, mat_imag, val_imag, precision=precise_mode
    )
    imag_out = jnp.einsum(formula, mat_real, val_imag, precision=precise_mode) + jnp.einsum(
        formula, mat_imag, val_real, precision=precise_mode
    )
    return (real_out, imag_out)


def factors(length_total):
    first_factor = 1
    for candidate in range(1, math.isqrt(length_total) + 1):
        if length_total % candidate == 0:
            first_factor = candidate
    return (first_factor, length_total // first_factor)


def combine_spectra(spec_real, spec_imag, width):
    filt_re = spec_real[..., :width]
    inner_re = spec_real[..., width : 2 * width]
    up_re = spec_real[..., 2 * width :]
    filt_im = spec_imag[..., :width]
    inner_im = spec_imag[..., width : 2 * width]
    up_im = spec_imag[..., 2 * width :]
    joined_real = jnp.concatenate(
        [
            filt_re * inner_re - filt_im * inner_im,
            filt_re * up_re + filt_im * up_im,
            up_re * inner_re + up_im * inner_im,
        ],
        axis=-1,
    )
    joined_imag = jnp.concatenate(
        [
            filt_re * inner_im + filt_im * inner_re,
            filt_re * up_im - filt_im * up_re,
            up_im * inner_re - up_re * inner_im,
        ],
        axis=-1,
    )
    return (joined_real, joined_imag)


def local_convolve(signals):
    length, branch_count, narrow = signals.shape
    total = 2 * length
    first_factor, second_factor = factors(total)
    flat = signals.reshape(length, branch_count * narrow)
    padded = jnp.concatenate([flat, jnp.zeros_like(flat)], axis=0).reshape(
        first_factor, second_factor, branch_count * narrow
    )
    first_index = jnp.arange(first_factor, dtype=jnp.int32)
    second_index = jnp.arange(second_factor, dtype=jnp.int32)
    cosine, sine_part = angles(first_index[:, None] * first_index[None, :], first_factor, -1.0)
    real_part = jnp.einsum("kn,nbm->kbm", cosine, padded, precision=precise_mode)
    imag_part = jnp.einsum("kn,nbm->kbm", sine_part, padded, precision=precise_mode)
    cosine, sine_part = angles(first_index[:, None] * second_index[None, :], total, -1.0)
    real_part, imag_part = rotate(real_part, imag_part, cosine[:, :, None], sine_part[:, :, None])
    real_part, imag_part = complex_einsum(
        "lb,kbm->klm",
        angles(second_index[:, None] * second_index[None, :], second_factor, -1.0),
        (real_part, imag_part),
    )
    real_part, imag_part = combine_spectra(real_part, imag_part, narrow)
    real_part, imag_part = complex_einsum(
        "bl,klm->kbm",
        angles(second_index[:, None] * second_index[None, :], second_factor, 1.0),
        (real_part, imag_part),
    )
    cosine, sine_part = angles(first_index[:, None] * second_index[None, :], total, 1.0)
    real_part, imag_part = rotate(real_part, imag_part, cosine[:, :, None], sine_part[:, :, None])
    cosine, sine_part = angles(first_index[:, None] * first_index[None, :], first_factor, 1.0)
    result = jnp.einsum("nk,kbm->nbm", cosine, real_part, precision=precise_mode) - jnp.einsum(
        "nk,kbm->nbm", sine_part, imag_part, precision=precise_mode
    )
    result = result.reshape(total, branch_count * narrow)[:length] / total
    return result.reshape(length, branch_count, narrow)


def shards(token_ids, embedding, proj_weight, filters, cotangent):
    tok_count = token_ids.shape[0]
    devices = lax.axis_size("seq")
    count = lax.axis_size("red")
    if fits_kernels(devices, count, token_ids, embedding, proj_weight, filters):
        return kernel_shards(
            devices, count, token_ids, embedding, proj_weight, filters, cotangent
        )
    width = filters.shape[1]
    vocabulary = embedding.shape[0]
    width_rows, branches, red_count, piece = proj_weight.shape
    scale_factor = float(tok_count * devices) ** (-0.5)
    table = jnp.dot(
        embedding,
        proj_weight.reshape(width_rows, branches * red_count * piece),
        preferred_element_type=jnp.float32,
    )
    table = table.reshape(vocabulary, branches, red_count, piece)
    own_table = lax.psum_scatter(table, "red", scatter_dimension=2, tiled=True)
    full_table = lax.all_gather(own_table, "seq", axis=3, tiled=True)
    projected = jnp.take(full_table, token_ids, axis=0)
    projected = projected.reshape(tok_count, branches, width)
    queries = projected[:, 0]
    key_rows = projected[:, 1]
    value_rows = projected[:, 2]
    inner = key_rows * value_rows
    upstream = cotangent * queries
    stacked = jnp.stack([filters, inner, upstream], axis=1)
    whole_length = lax.all_to_all(stacked, "seq", split_axis=2, concat_axis=0, tiled=True)
    results = local_convolve(whole_length)
    returned = lax.all_to_all(results, "seq", split_axis=0, concat_axis=2, tiled=True)
    conv = returned[:, 0]
    grad_inner = returned[:, 1]
    filter_raw = returned[:, 2]
    output = queries * conv
    filter_grad = filter_raw * scale_factor
    branch_grads = jnp.stack(
        [cotangent * conv, grad_inner * value_rows, grad_inner * key_rows], axis=1
    ).astype(jnp.bfloat16)
    one_hot = (token_ids[:, None] == lax.iota(jnp.int32, vocabulary)[None, :]).astype(jnp.bfloat16)
    token_sums = lax.dot_general(
        one_hot,
        branch_grads.reshape(tok_count, branches * width),
        (((0,), (0,)), ((), ())),
        preferred_element_type=jnp.float32,
    )
    summed = lax.psum_scatter(
        token_sums.reshape(vocabulary, branches, width), "seq", scatter_dimension=2, tiled=True
    )
    gathered = lax.all_gather(summed[:, :, None, :], "red", axis=2, tiled=True)
    weight_grad = (
        lax.dot_general(
            embedding.astype(jnp.float32),
            gathered.reshape(vocabulary, branches * red_count * piece),
            (((0,), (0,)), ((), ())),
            precision=precise_mode,
        )
        * scale_factor
    )
    return (
        output,
        filter_grad,
        branch_grads,
        weight_grad.reshape(width_rows, branches, red_count, piece),
    )


def solution(mesh):
    in_specs = (
        P("seq"),
        P(None, "red"),
        P("red", None, None, "seq"),
        P("seq", "red"),
        P("seq", "red"),
    )
    out_specs = (
        P("seq", "red"),
        P("seq", "red"),
        P("seq", None, "red"),
        P("red", None, None, "seq"),
    )
    return jax.shard_map(shards, mesh=mesh, in_specs=in_specs, out_specs=out_specs, check_vma=False)
```

```python
import functools
import math

import jax
import jax.numpy as jnp
import numpy as np
from jax import lax
from jax.experimental import pallas as pl
from jax.experimental.pallas import tpu as pltpu
from jax.sharding import PartitionSpec as P

precise_mode = lax.Precision.HIGHEST
MESH = pl.DeviceIdType.MESH
VMEM = pl.BlockSpec(memory_space=pltpu.VMEM)
SHARES = (1, 1)
REDUCE_DIRECT = (False, True)
PIECES = 3
VMEM_BYTES = 67043328
NN = (((1,), (0,)), ((), ()))
NT = (((1,), (1,)), ((), ()))


def dot(left, right, dims=NN):
    return lax.dot_general(left, right, dims, preferred_element_type=jnp.float32)


def stack_split(value):
    high = value.astype(jnp.bfloat16).astype(jnp.float32)
    return jnp.concatenate([high, value - high], axis=0).astype(jnp.bfloat16)


def dot_split(value, matrix, dims=NN):
    both = dot(stack_split(value), matrix, dims)
    rows = value.shape[0]
    return both[:rows] + both[rows:]


def dot_both(value, matrix_high, matrix_low, dims=NN):
    high = value.astype(jnp.bfloat16)
    return dot_split(value, matrix_high, dims) + dot(high, matrix_low, dims)


def transform_tables(block, blocks):
    total = 2 * blocks * block
    place = np.arange(block)
    half = block // 2
    tables = np.zeros((2, 2 * block, 2 * block))
    even = 2 * np.pi * ((2 * blocks * place[:, None] * np.arange(half)[None, :]) % total) / total
    odd = 2 * np.pi * ((place[:, None] * (blocks + 2 * blocks * np.arange(half))[None, :]) % total) / total
    tables[0, :block, :half] = np.cos(even)
    tables[0, :block, block : block + half] = np.sin(even)
    tables[0, :block, block] = 1.0 - 2.0 * (place % 2)
    tables[0, block:, half:block] = np.cos(odd)
    tables[0, block:, block + half :] = np.sin(odd)
    psi = 2 * np.pi * ((place[:, None] * place[None, :]) % block) / block
    tables[1, :block, :block] = np.cos(psi)
    tables[1, :block, block:] = np.sin(psi)
    tables[1, block:, :block] = -np.sin(psi)
    tables[1, block:, block:] = np.cos(psi)
    tables = tables.astype(np.float32)
    high = tables.astype(jnp.bfloat16)
    low = (tables - high.astype(np.float32)).astype(jnp.bfloat16)
    alpha = 2 * np.pi * np.arange(blocks)[:, None] * place[None, :] / total
    return high, low, np.concatenate([np.cos(alpha), np.sin(alpha)]).astype(np.float32)


def phases(residue, blocks):
    if residue == 0:
        return [1.0] * blocks, [(-1.0) ** index for index in range(blocks)]
    turn = [math.pi * ((residue * index) % (2 * blocks)) / blocks for index in range(blocks)]
    return [math.cos(a) for a in turn], [math.sin(a) for a in turn]


def weighted(terms, weights):
    total = None
    for term, weight in zip(terms, weights):
        if abs(weight) < 1e-12:
            continue
        part = term if weight == 1.0 else (-term if weight == -1.0 else term * weight)
        total = part if total is None else total + part
    return total


def fold(pieces, residue, blocks):
    cosines, sines = phases(residue, blocks)
    return weighted(pieces, cosines), weighted(pieces, sines)


def combine(spectrum, block, sub, first):
    cos_part = spectrum[:, :block]
    sin_part = spectrum[:, block:]
    fc, ic, uc = (cos_part[at * sub : (at + 1) * sub] for at in range(3))
    fs, i_s, us = (sin_part[at * sub : (at + 1) * sub] for at in range(3))
    cc = [fc * ic, fc * uc, uc * ic]
    ss = [fs * i_s, fs * us, us * i_s]
    new_cos = [cc[0] - ss[0], cc[1] + ss[1], cc[2] + ss[2]]
    new_sin = [fc * i_s + fs * ic, fc * us - fs * uc, us * ic - uc * i_s]
    new_cos = jnp.concatenate(new_cos, axis=0)
    new_sin = jnp.concatenate(new_sin, axis=0)
    if first:
        lane = lax.broadcasted_iota(jnp.int32, new_cos.shape, 1) == 0
        new_cos = jnp.where(lane, 0.5 * jnp.concatenate(cc, axis=0), new_cos)
        new_sin = jnp.where(lane, 0.5 * jnp.concatenate(ss, axis=0), new_sin)
    return jnp.concatenate([new_cos, new_sin], axis=1)


def convolve(pieces, high_ref, low_ref, turn_ref, sub):
    blocks = len(pieces)
    block = pieces[0].shape[1]
    rows = 3 * sub
    scale = 1.0 / (blocks * block)
    turns = [(turn_ref[at : at + 1], turn_ref[blocks + at : blocks + at + 1]) for at in range(blocks)]
    first = dot_both(jnp.concatenate(fold(pieces, 0, blocks), axis=1), high_ref[0], low_ref[0])
    packed = []
    for residue in range(1, blocks):
        even, odd = fold(pieces, residue, blocks)
        cosine, sine = turns[residue]
        packed.append(
            jnp.concatenate([even * cosine - odd * sine, even * sine + odd * cosine], axis=1)
        )
    spectrum = dot_both(jnp.concatenate(packed, axis=0), high_ref[1], low_ref[1])
    joined = [
        combine(spectrum[at * rows : (at + 1) * rows], block, sub, False) * scale
        for at in range(blocks - 1)
    ]
    head = dot_both(combine(first, block, sub, True) * scale, high_ref[0], low_ref[0], NT)
    back = dot_both(jnp.concatenate(joined, axis=0), high_ref[1], low_ref[1], NT)
    cosines, sines = phases(0, blocks)
    results = [
        weighted([head[:, :block], head[:, block:]], [cosines[at], sines[at]])
        for at in range(blocks)
    ]
    for residue in range(1, blocks):
        real = back[(residue - 1) * rows : residue * rows, :block]
        imag = back[(residue - 1) * rows : residue * rows, block:]
        cosine, sine = turns[residue]
        cosines, sines = phases(residue, blocks)
        pair = [real * cosine + imag * sine, imag * cosine - real * sine]
        for at in range(blocks):
            results[at] = results[at] + weighted(pair, [cosines[at], sines[at]])
    return results


def partners(count):
    spot = lax.axis_index("red")
    return spot + 1 - 2 * lax.rem(spot, 2), count - 1 - spot


def greet(devices, count):
    me = lax.axis_index("seq")
    barrier = pltpu.get_barrier_semaphore()
    for step in range(1, devices):
        peer = lax.rem(me + step, devices)
        pl.semaphore_signal(barrier, inc=1, device_id={"seq": peer}, device_id_type=MESH)
    for partner in partners(count):
        pl.semaphore_signal(barrier, inc=1, device_id={"red": partner}, device_id_type=MESH)


def meet(devices, count):
    pl.semaphore_wait(pltpu.get_barrier_semaphore(), devices - 1 + len(partners(count)))


def remote(source, target, send_sem, recv_sem, **where):
    return pltpu.make_async_remote_copy(
        src_ref=source,
        dst_ref=target,
        send_sem=send_sem,
        recv_sem=recv_sem,
        device_id=where,
        device_id_type=MESH,
    )


def exchange(devices, source, target, send_sem, recv_sem):
    me = lax.axis_index("seq")
    for step in range(1, devices):
        peer = lax.rem(me + step, devices)
        remote(source(peer), target(me), send_sem, recv_sem, seq=peer).start()


def semaphores(chunks, count):
    counts = {
        "load": 7 + count, "signals": 2, "answers": 2, "reduce": 1, "gather": 1,
        "same0": chunks * PIECES, "same1": chunks, "same2": chunks * PIECES,
        "cross0": chunks * PIECES, "cross1": chunks,
        "near": chunks * PIECES, "far": chunks * PIECES, "relay": chunks,
    }
    bases, total = {}, 0
    for name, needed in counts.items():
        bases[name] = total
        total += needed
    return bases, total


def chunk_sizes(piece):
    return [piece * share // sum(SHARES) for share in SHARES]


def main_kernel(
    devices, count, scale_factor,
    tok_hbm, emb_hbm, wt_hbm, filt_hbm, cot_hbm, high_hbm, low_hbm, turn_hbm,
    out_ref, fgrad_ref, grads_ref, weight_ref,
    tok_ref, emb_ref, wt_ref, filt_ref, cot_ref, high_ref, low_ref, turn_ref,
    part, from_same, from_cross, all_ref, out_sig, sig, sending, recv, one_hot,
    sems,
):
    me = lax.axis_index("seq")
    spot = lax.axis_index("red")
    branches, _, piece, _ = wt_ref.shape
    tok_count, width = filt_ref.shape
    vocabulary = emb_ref.shape[0]
    sizes = chunk_sizes(piece)
    starts = [sum(sizes[:at]) for at in range(len(sizes))]
    chunks = len(sizes)
    last = count - 1
    same, cross = partners(count)
    bases, _ = semaphores(chunks, count)

    def sem(name, index=0):
        return sems.at[bases[name] + index]

    low_half = spot * 2 < count
    end = jnp.where(low_half, 0, last)
    middle = jnp.where(low_half, 1, last - 1)
    far_middle = last - middle
    far_end = last - end
    outer = spot == end
    inner = spot == middle
    greet(devices, count)

    def pick(at_end, at_middle):
        return jnp.where(outer, at_end, at_middle)

    orders = [
        pick(far_middle if REDUCE_DIRECT[0] else far_end, far_end),
        pick(far_end if REDUCE_DIRECT[0] else far_middle, far_middle),
        pick(middle, end),
        spot,
    ]

    def goal_at(index):
        return orders[index]

    def load(index, source, target):
        copy = pltpu.make_async_copy(source, target, sem("load", index))
        copy.start()
        return copy

    emb_load = load(0, emb_hbm, emb_ref)
    wt_loads = []
    for index in range(count):
        goal = goal_at(index)
        wt_loads.append(load(7 + index, wt_hbm.at[:, goal], wt_ref.at[:, goal]))
    signal_loads = [
        load(1, filt_hbm, filt_ref), load(2, cot_hbm, cot_ref), load(3, tok_hbm, tok_ref),
    ]
    table_loads = [
        load(4, high_hbm, high_ref), load(5, low_hbm, low_ref), load(6, turn_hbm, turn_ref),
    ]
    def view(ref, chunk, group, at=None):
        rows = branches * sizes[chunk]
        base = branches * starts[chunk]
        if at is not None:
            rows //= PIECES
            base += at * rows
        return ref.at[group, pl.ds(base, rows)]

    def slot(name, chunk, at):
        if name in ("same1", "cross1", "relay"):
            return sem(name, chunk)
        return sem(name, chunk * PIECES + at)

    def to_same(kind, chunk, group, at=None):
        return remote(
            view(part, chunk, group, at), view(from_same, chunk, group, at),
            sem("reduce"), slot(f"same{kind}", chunk, at), red=same,
        )

    def to_cross(kind, chunk, group, at=None):
        return remote(
            view(part, chunk, group, at), view(from_cross, chunk, group, at),
            sem("reduce"), slot(f"cross{kind}", chunk, at), red=cross,
        )

    def share_to(name, chunk, group, at, partner):
        block = view(all_ref, chunk, group, at)
        return remote(block, block, sem("gather"), slot(name, chunk, at), red=partner)

    def every(make, kind, chunk, group):
        for at in range(PIECES):
            make(kind, chunk, group, at).start()

    def add(source, chunk, group, at):
        piece_ref = view(part, chunk, group, at)
        piece_ref[...] = piece_ref[...] + view(source, chunk, group, at)[...]

    def products(index):
        goal = goal_at(index)
        wt_loads[index].wait()
        rows = jnp.concatenate([wt_ref[b, goal] for b in range(branches)], axis=0)
        product = dot(rows, emb_ref[...], NT)
        for start, size in zip(starts, sizes):
            for b in range(branches):
                base = branches * start + b * size
                part[goal, base : base + size] = product[b * piece + start : b * piece + start + size]

    def first_sends(chunk, index):
        direct = REDUCE_DIRECT[chunk]
        if index == 0:
            @pl.when(outer)
            def _():
                if direct:
                    every(to_same, 0, chunk, far_middle)
                else:
                    every(to_same, 2, chunk, far_end)

            if direct:
                @pl.when(inner)
                def _():
                    every(to_cross, 0, chunk, far_end)

        if index == 1:
            @pl.when(outer)
            def _():
                if direct:
                    every(to_cross, 0, chunk, far_end)
                else:
                    every(to_same, 0, chunk, far_middle)

        if index == 2:
            @pl.when(outer)
            def _():
                every(to_same, 1, chunk, middle)

    def pass_far(chunk, at):
        to_same(2, chunk, far_end, at).wait_recv()
        add(from_same, chunk, far_end, at)
        to_cross(0, chunk, far_end, at).start()

    def pass_cross(chunk, at):
        to_same(0, chunk, far_middle, at).wait_recv()
        add(from_same, chunk, far_middle, at)
        to_cross(1, chunk, far_middle, at).start()

    def pass_same(chunk, at):
        to_cross(0, chunk, end, at).wait_recv()
        add(from_cross, chunk, end, at)
        to_same(0, chunk, end, at).start()

    def arrive(chunk):
        @pl.when(inner)
        def _():
            to_same(1, chunk, spot).wait_recv()
            to_cross(1, chunk, spot).wait_recv()

        @pl.when(outer)
        def _():
            for at in range(PIECES):
                to_same(0, chunk, spot, at).wait_recv()
                if REDUCE_DIRECT[chunk]:
                    to_cross(0, chunk, spot, at).wait_recv()

        own = view(part, chunk, spot)[...] + view(from_same, chunk, spot)[...]
        crossed = view(from_cross, chunk, spot)
        if REDUCE_DIRECT[chunk]:
            return own + crossed[...]

        @pl.when(outer)
        def _():
            crossed[...] = jnp.zeros(crossed.shape, jnp.float32)

        return own + crossed[...]

    def share(chunk):
        for at in range(PIECES):
            share_to("near", chunk, spot, at, same).start()
        for at in range(PIECES):
            share_to("far", chunk, spot, at, cross).start()

    def relay_same(chunk, at):
        share_to("far", chunk, far_middle, at, cross).wait_recv()
        share_to("relay", chunk, far_middle, at, same).start()

    def relay_cross(chunk, at):
        share_to("near", chunk, end, at, same).wait_recv()
        share_to("relay", chunk, end, at, cross).start()

    def collect(name, group, role):
        @pl.when(role)
        def _():
            for chunk in range(chunks):
                for at in [None] if name == "relay" else range(PIECES):
                    share_to(name, chunk, group, at, same).wait_recv()

    def weights(group):
        product = dot_split(all_ref[group], emb_ref[...]) * scale_factor
        for start, size in zip(starts, sizes):
            for b in range(branches):
                base = branches * start + b * size
                weight_ref[b, group, start : start + size] = product[base : base + size]

    def signal_rows(start, rows, at):
        return sig[at, start : start + rows]

    def channels(chunk, own, hook):
        start, size = starts[chunk], sizes[chunk]
        projected = dot_split(own, one_hot[...])
        pieces = []
        held = []
        for at in range(devices):
            block = projected[:, at * tok_count : (at + 1) * tok_count]
            queries, key_rows, value_rows = (block[b * size : (b + 1) * size] for b in range(3))
            cotangent = signal_rows(piece + start, size, at)
            held.append((queries, key_rows, value_rows, cotangent))
            pieces.append(
                jnp.concatenate(
                    [signal_rows(start, size, at), key_rows * value_rows, cotangent * queries], axis=0
                )
            )
        results = convolve(pieces, high_ref, low_ref, turn_ref, size)
        hook()
        rounded = []
        for at in range(devices):
            queries, key_rows, value_rows, cotangent = held[at]
            conv = results[at][:size]
            grad_inner = results[at][size : 2 * size]
            grads = jnp.concatenate(
                [cotangent * conv, grad_inner * value_rows, grad_inner * key_rows], axis=0
            ).astype(jnp.bfloat16)
            rounded.append(grads)
            base = 5 * start
            sending[at, base : base + size] = queries * conv
            sending[at, base + size : base + 2 * size] = results[at][2 * size :] * scale_factor
            sending[at, base + 2 * size : base + 5 * size] = grads.astype(jnp.float32)
        sums = dot(jnp.concatenate(rounded, axis=1), one_hot[...], NT)
        view(all_ref, chunk, spot)[...] = sums

    def positions(at):
        parts = [
            recv[peer, 5 * start + at * size : 5 * start + (at + 1) * size]
            for peer in range(devices)
            for start, size in zip(starts, sizes)
        ]
        return jnp.concatenate(parts, axis=0).T

    emb_load.wait()
    products(0)
    meet(devices, count)
    first_sends(0, 0)
    for copy in signal_loads:
        copy.wait()
    filt_t = filt_ref[...].T
    cot_t = cot_ref[...].T
    tok_rows = jnp.broadcast_to(tok_ref[...].astype(jnp.float32), (8, tok_count))
    for peer in range(devices):
        out_sig[peer, :piece] = filt_t[peer * piece : (peer + 1) * piece]
        out_sig[peer, piece : 2 * piece] = cot_t[peer * piece : (peer + 1) * piece]
        out_sig[peer, 2 * piece :] = tok_rows
    exchange(devices, out_sig.at.__getitem__, sig.at.__getitem__, sem("signals"), sem("signals", 1))
    for index in range(1, count):
        products(index)
        first_sends(0, index)
    for index in range(count):
        first_sends(1, index)
    sig[me] = out_sig[me]
    others = pl.ds(0, devices - 1)
    signals = remote(out_sig.at[others], sig.at[others], sem("signals"), sem("signals", 1), red=same)
    answers = remote(sending.at[others], recv.at[others], sem("answers"), sem("answers", 1), red=same)

    @pl.when(inner)
    def _():
        if REDUCE_DIRECT[0]:
            for at in range(PIECES):
                pass_cross(0, at)
                pass_same(0, at)
        else:
            for at in range(PIECES):
                pass_far(0, at)
            for at in range(PIECES):
                pass_same(0, at)
                pass_cross(0, at)
        if REDUCE_DIRECT[1]:
            for at in range(PIECES):
                pass_same(1, at)

    signals.wait_recv()
    ids = jnp.concatenate([signal_rows(2 * piece, 1, at) for at in range(devices)], axis=1)
    vocab_rows = lax.broadcasted_iota(jnp.int32, (vocabulary, devices * tok_count), 0)
    one_hot[...] = jnp.where(vocab_rows == ids.astype(jnp.int32), 1.0, 0.0).astype(jnp.bfloat16)
    for copy in table_loads:
        copy.wait()

    def reduce_hook():
        @pl.when(inner)
        def _():
            if REDUCE_DIRECT[1]:
                for at in range(PIECES):
                    pass_cross(1, at)
            else:
                for at in range(PIECES):
                    pass_far(1, at)

    def gather_hook():
        @pl.when(inner)
        def _():
            for at in range(PIECES):
                relay_same(0, at)

    for chunk, hook in enumerate([reduce_hook, gather_hook]):
        if chunk == 1 and not REDUCE_DIRECT[1]:
            @pl.when(inner)
            def _():
                for at in range(PIECES):
                    pass_same(1, at)
                    pass_cross(1, at)

        channels(chunk, arrive(chunk), hook)
        share(chunk)
        rows = pl.ds(5 * starts[chunk], 5 * sizes[chunk])
        exchange(
            devices,
            lambda peer, rows=rows: sending.at[peer, rows],
            lambda slot, rows=rows: recv.at[slot, rows],
            sem("answers"), sem("answers", 1),
        )
        recv[me, 5 * starts[chunk] : 5 * (starts[chunk] + sizes[chunk])] = sending[
            me, 5 * starts[chunk] : 5 * (starts[chunk] + sizes[chunk])
        ]

    @pl.when(inner)
    def _():
        for at in range(PIECES):
            relay_cross(0, at)

    weights(spot)

    @pl.when(inner)
    def _():
        for at in range(PIECES):
            relay_cross(1, at)
            relay_same(1, at)

    answers.wait_recv()
    out_ref[...] = positions(0)
    fgrad_ref[...] = positions(1)
    for branch in range(branches):
        grads_ref[branch] = positions(2 + branch).astype(jnp.bfloat16)
    collect("near", middle, outer)
    weights(pick(middle, end))
    collect("far", far_end, outer)
    weights(pick(far_end, far_middle))
    collect("relay", pick(far_middle, far_end), outer | inner)
    weights(pick(far_middle, far_end))
    reduced = pl.ds(0, last)
    remote(part.at[reduced], from_same.at[reduced], sem("reduce"), sem("same0"), red=same).wait_send()

    @pl.when(outer)
    def _():
        pair = all_ref.at[pl.ds(0, 2)]
        remote(pair, pair, sem("gather"), sem("near"), red=same).wait_send()

    @pl.when(inner)
    def _():
        remote(all_ref, all_ref, sem("gather"), sem("near"), red=same).wait_send()

    signals.wait_send()
    answers.wait_send()


def final_kernel(out_in, fgrad_in, grads_in, weight_in, out_ref, fgrad_ref, grads_ref, weight_ref, sem):
    pairs = [(weight_in, weight_ref), (grads_in, grads_ref), (out_in, out_ref), (fgrad_in, fgrad_ref)]
    copies = [
        pltpu.make_async_copy(source, target, sem.at[index])
        for index, (source, target) in enumerate(pairs)
    ]
    for copy in copies:
        copy.start()
    for copy in copies:
        copy.wait()


def kernel_shards(devices, count, token_ids, embedding, proj_weight, filters, cotangent):
    tok_count, width = filters.shape
    vocabulary, depth = embedding.shape
    _, branches, _, piece = proj_weight.shape
    scale_factor = float(tok_count * devices) ** (-0.5)
    chunks = len(SHARES)
    f32 = jnp.float32
    bf16 = jnp.bfloat16
    dma = pltpu.SemaphoreType.DMA
    weight_t = jnp.transpose(proj_weight, (1, 2, 3, 0))
    high, low, turn = transform_tables(tok_count, devices)
    block = (count, branches * piece, vocabulary)
    message = (devices, 2 * piece + 8, tok_count)
    answer = (devices, 5 * piece, tok_count)
    results = (
        ((tok_count, width), f32),
        ((tok_count, width), f32),
        ((branches, tok_count, width), bf16),
        ((branches, count, piece, depth), f32),
    )
    kept = sum(math.prod(shape) * jnp.dtype(kind).itemsize for shape, kind in results) + 2**17
    held = pl.pallas_call(
        functools.partial(main_kernel, devices, count, scale_factor),
        out_shape=tuple(pltpu.VMEM(shape, kind) for shape, kind in results),
        in_specs=[pl.BlockSpec(memory_space=pltpu.HBM)] * 8,
        out_specs=(VMEM,) * 4,
        scratch_shapes=[
            pltpu.VMEM((1, tok_count), jnp.int32),
            pltpu.VMEM(embedding.shape, bf16),
            pltpu.VMEM(weight_t.shape, bf16),
            pltpu.VMEM(filters.shape, f32),
            pltpu.VMEM(cotangent.shape, f32),
            pltpu.VMEM(high.shape, bf16),
            pltpu.VMEM(low.shape, bf16),
            pltpu.VMEM(turn.shape, f32),
            pltpu.VMEM(block, f32),
            pltpu.VMEM(block, f32),
            pltpu.VMEM(block, f32),
            pltpu.VMEM(block, f32),
            pltpu.VMEM(message, f32),
            pltpu.VMEM(message, f32),
            pltpu.VMEM(answer, f32),
            pltpu.VMEM(answer, f32),
            pltpu.VMEM((vocabulary, devices * tok_count), bf16),
            dma((semaphores(chunks, count)[1],)),
        ],
        compiler_params=pltpu.CompilerParams(
            collective_id=0, has_side_effects=True, vmem_limit_bytes=VMEM_BYTES - kept
        ),
        name="hyena_exchange",
    )(
        token_ids.reshape(1, tok_count), embedding, weight_t, filters, cotangent,
        jnp.asarray(high), jnp.asarray(low), jnp.asarray(turn),
    )
    output, filter_grad, grads, weight = pl.pallas_call(
        final_kernel,
        out_shape=tuple(jax.ShapeDtypeStruct(shape, kind) for shape, kind in results),
        in_specs=[VMEM] * 4,
        out_specs=(pl.BlockSpec(memory_space=pltpu.HBM),) * 4,
        scratch_shapes=[dma((4,))],
        compiler_params=pltpu.CompilerParams(vmem_limit_bytes=2**20),
        name="finish",
    )(*held)
    return (
        output,
        filter_grad,
        jnp.transpose(grads, (1, 0, 2)),
        jnp.transpose(weight, (3, 0, 1, 2)),
    )


def fits_kernels(devices, count, token_ids, embedding, proj_weight, filters):
    tok_count, width = filters.shape
    vocabulary, depth = embedding.shape
    _, branches, red_count, piece = proj_weight.shape
    lanes = (tok_count, vocabulary, depth)
    aligned = all(size % 128 == 0 for size in lanes) and piece % (8 * sum(SHARES)) == 0 and branches * piece % (8 * sum(SHARES) * PIECES) == 0
    one_hot = vocabulary * tok_count * devices * 8
    held = 4 * branches * piece * (4 * count * vocabulary + 2 * count * depth)
    sides = 4 * tok_count * devices * 20 * piece + 16 * vocabulary * depth
    return (
        aligned
        and count == 4
        and branches == 3
        and red_count == count
        and width == devices * piece
        and one_hot + held + sides < 36 * 2**20
    )


def angles(numbers, modulus, direction):
    phase = (numbers % modulus).astype(jnp.float32) * (direction * 2.0 * math.pi / modulus)
    return (jnp.cos(phase), jnp.sin(phase))


def rotate(real_part, imag_part, cosine, sine_part):
    return (real_part * cosine - imag_part * sine_part, real_part * sine_part + imag_part * cosine)


def complex_einsum(formula, matrix, values):
    mat_real, mat_imag = matrix
    val_real, val_imag = values
    real_out = jnp.einsum(formula, mat_real, val_real, precision=precise_mode) - jnp.einsum(
        formula, mat_imag, val_imag, precision=precise_mode
    )
    imag_out = jnp.einsum(formula, mat_real, val_imag, precision=precise_mode) + jnp.einsum(
        formula, mat_imag, val_real, precision=precise_mode
    )
    return (real_out, imag_out)


def factors(length_total):
    first_factor = 1
    for candidate in range(1, math.isqrt(length_total) + 1):
        if length_total % candidate == 0:
            first_factor = candidate
    return (first_factor, length_total // first_factor)


def combine_spectra(spec_real, spec_imag, width):
    filt_re = spec_real[..., :width]
    inner_re = spec_real[..., width : 2 * width]
    up_re = spec_real[..., 2 * width :]
    filt_im = spec_imag[..., :width]
    inner_im = spec_imag[..., width : 2 * width]
    up_im = spec_imag[..., 2 * width :]
    joined_real = jnp.concatenate(
        [
            filt_re * inner_re - filt_im * inner_im,
            filt_re * up_re + filt_im * up_im,
            up_re * inner_re + up_im * inner_im,
        ],
        axis=-1,
    )
    joined_imag = jnp.concatenate(
        [
            filt_re * inner_im + filt_im * inner_re,
            filt_re * up_im - filt_im * up_re,
            up_im * inner_re - up_re * inner_im,
        ],
        axis=-1,
    )
    return (joined_real, joined_imag)


def local_convolve(signals):
    length, branch_count, narrow = signals.shape
    total = 2 * length
    first_factor, second_factor = factors(total)
    flat = signals.reshape(length, branch_count * narrow)
    padded = jnp.concatenate([flat, jnp.zeros_like(flat)], axis=0).reshape(
        first_factor, second_factor, branch_count * narrow
    )
    first_index = jnp.arange(first_factor, dtype=jnp.int32)
    second_index = jnp.arange(second_factor, dtype=jnp.int32)
    cosine, sine_part = angles(first_index[:, None] * first_index[None, :], first_factor, -1.0)
    real_part = jnp.einsum("kn,nbm->kbm", cosine, padded, precision=precise_mode)
    imag_part = jnp.einsum("kn,nbm->kbm", sine_part, padded, precision=precise_mode)
    cosine, sine_part = angles(first_index[:, None] * second_index[None, :], total, -1.0)
    real_part, imag_part = rotate(real_part, imag_part, cosine[:, :, None], sine_part[:, :, None])
    real_part, imag_part = complex_einsum(
        "lb,kbm->klm",
        angles(second_index[:, None] * second_index[None, :], second_factor, -1.0),
        (real_part, imag_part),
    )
    real_part, imag_part = combine_spectra(real_part, imag_part, narrow)
    real_part, imag_part = complex_einsum(
        "bl,klm->kbm",
        angles(second_index[:, None] * second_index[None, :], second_factor, 1.0),
        (real_part, imag_part),
    )
    cosine, sine_part = angles(first_index[:, None] * second_index[None, :], total, 1.0)
    real_part, imag_part = rotate(real_part, imag_part, cosine[:, :, None], sine_part[:, :, None])
    cosine, sine_part = angles(first_index[:, None] * first_index[None, :], first_factor, 1.0)
    result = jnp.einsum("nk,kbm->nbm", cosine, real_part, precision=precise_mode) - jnp.einsum(
        "nk,kbm->nbm", sine_part, imag_part, precision=precise_mode
    )
    result = result.reshape(total, branch_count * narrow)[:length] / total
    return result.reshape(length, branch_count, narrow)


def shards(token_ids, embedding, proj_weight, filters, cotangent):
    tok_count = token_ids.shape[0]
    devices = lax.axis_size("seq")
    count = lax.axis_size("red")
    if fits_kernels(devices, count, token_ids, embedding, proj_weight, filters):
        return kernel_shards(
            devices, count, token_ids, embedding, proj_weight, filters, cotangent
        )
    width = filters.shape[1]
    vocabulary = embedding.shape[0]
    width_rows, branches, red_count, piece = proj_weight.shape
    scale_factor = float(tok_count * devices) ** (-0.5)
    table = jnp.dot(
        embedding,
        proj_weight.reshape(width_rows, branches * red_count * piece),
        preferred_element_type=jnp.float32,
    )
    table = table.reshape(vocabulary, branches, red_count, piece)
    own_table = lax.psum_scatter(table, "red", scatter_dimension=2, tiled=True)
    full_table = lax.all_gather(own_table, "seq", axis=3, tiled=True)
    projected = jnp.take(full_table, token_ids, axis=0)
    projected = projected.reshape(tok_count, branches, width)
    queries = projected[:, 0]
    key_rows = projected[:, 1]
    value_rows = projected[:, 2]
    inner = key_rows * value_rows
    upstream = cotangent * queries
    stacked = jnp.stack([filters, inner, upstream], axis=1)
    whole_length = lax.all_to_all(stacked, "seq", split_axis=2, concat_axis=0, tiled=True)
    results = local_convolve(whole_length)
    returned = lax.all_to_all(results, "seq", split_axis=0, concat_axis=2, tiled=True)
    conv = returned[:, 0]
    grad_inner = returned[:, 1]
    filter_raw = returned[:, 2]
    output = queries * conv
    filter_grad = filter_raw * scale_factor
    branch_grads = jnp.stack(
        [cotangent * conv, grad_inner * value_rows, grad_inner * key_rows], axis=1
    ).astype(jnp.bfloat16)
    one_hot = (token_ids[:, None] == lax.iota(jnp.int32, vocabulary)[None, :]).astype(jnp.bfloat16)
    token_sums = lax.dot_general(
        one_hot,
        branch_grads.reshape(tok_count, branches * width),
        (((0,), (0,)), ((), ())),
        preferred_element_type=jnp.float32,
    )
    summed = lax.psum_scatter(
        token_sums.reshape(vocabulary, branches, width), "seq", scatter_dimension=2, tiled=True
    )
    gathered = lax.all_gather(summed[:, :, None, :], "red", axis=2, tiled=True)
    weight_grad = (
        lax.dot_general(
            embedding.astype(jnp.float32),
            gathered.reshape(vocabulary, branches * red_count * piece),
            (((0,), (0,)), ((), ())),
            precision=precise_mode,
        )
        * scale_factor
    )
    return (
        output,
        filter_grad,
        branch_grads,
        weight_grad.reshape(width_rows, branches, red_count, piece),
    )


def solution(mesh):
    in_specs = (
        P("seq"),
        P(None, "red"),
        P("red", None, None, "seq"),
        P("seq", "red"),
        P("seq", "red"),
    )
    out_specs = (
        P("seq", "red"),
        P("seq", "red"),
        P("seq", None, "red"),
        P("red", None, None, "seq"),
    )
    return jax.shard_map(shards, mesh=mesh, in_specs=in_specs, out_specs=out_specs, check_vma=False)
```

```python
import functools
import math

import jax
import jax.numpy as jnp
import numpy as np
from jax import lax
from jax.experimental import pallas as pl
from jax.experimental.pallas import tpu as pltpu
from jax.sharding import PartitionSpec as P

precise_mode = lax.Precision.HIGHEST
MESH = pl.DeviceIdType.MESH
VMEM = pl.BlockSpec(memory_space=pltpu.VMEM)
SHARES = (1, 1)
REDUCE_DIRECT = (False, True)
EARLY = True
ORDERB = True
STAGE = True
HOOK = 'after'
FARFIRST = (0, 1)
PIECES = 3
VMEM_BYTES = 67043328
NN = (((1,), (0,)), ((), ()))
NT = (((1,), (1,)), ((), ()))


def dot(left, right, dims=NN):
    return lax.dot_general(left, right, dims, preferred_element_type=jnp.float32)


def stack_split(value):
    high = value.astype(jnp.bfloat16).astype(jnp.float32)
    return jnp.concatenate([high, value - high], axis=0).astype(jnp.bfloat16)


def dot_split(value, matrix, dims=NN):
    both = dot(stack_split(value), matrix, dims)
    rows = value.shape[0]
    return both[:rows] + both[rows:]


def dot_both(value, matrix_high, matrix_low, dims=NN):
    high = value.astype(jnp.bfloat16)
    return dot_split(value, matrix_high, dims) + dot(high, matrix_low, dims)


def transform_tables(block, blocks):
    total = 2 * blocks * block
    place = np.arange(block)
    half = block // 2
    tables = np.zeros((2, 2 * block, 2 * block))
    even = 2 * np.pi * ((2 * blocks * place[:, None] * np.arange(half)[None, :]) % total) / total
    odd = 2 * np.pi * ((place[:, None] * (blocks + 2 * blocks * np.arange(half))[None, :]) % total) / total
    tables[0, :block, :half] = np.cos(even)
    tables[0, :block, block : block + half] = np.sin(even)
    tables[0, :block, block] = 1.0 - 2.0 * (place % 2)
    tables[0, block:, half:block] = np.cos(odd)
    tables[0, block:, block + half :] = np.sin(odd)
    psi = 2 * np.pi * ((place[:, None] * place[None, :]) % block) / block
    tables[1, :block, :block] = np.cos(psi)
    tables[1, :block, block:] = np.sin(psi)
    tables[1, block:, :block] = -np.sin(psi)
    tables[1, block:, block:] = np.cos(psi)
    tables = tables.astype(np.float32)
    high = tables.astype(jnp.bfloat16)
    low = (tables - high.astype(np.float32)).astype(jnp.bfloat16)
    alpha = 2 * np.pi * np.arange(blocks)[:, None] * place[None, :] / total
    return high, low, np.concatenate([np.cos(alpha), np.sin(alpha)]).astype(np.float32)


def phases(residue, blocks):
    if residue == 0:
        return [1.0] * blocks, [(-1.0) ** index for index in range(blocks)]
    turn = [math.pi * ((residue * index) % (2 * blocks)) / blocks for index in range(blocks)]
    return [math.cos(a) for a in turn], [math.sin(a) for a in turn]


def weighted(terms, weights):
    total = None
    for term, weight in zip(terms, weights):
        if abs(weight) < 1e-12:
            continue
        part = term if weight == 1.0 else (-term if weight == -1.0 else term * weight)
        total = part if total is None else total + part
    return total


def fold(pieces, residue, blocks):
    cosines, sines = phases(residue, blocks)
    return weighted(pieces, cosines), weighted(pieces, sines)


def combine(spectrum, block, sub, first):
    cos_part = spectrum[:, :block]
    sin_part = spectrum[:, block:]
    fc, ic, uc = (cos_part[at * sub : (at + 1) * sub] for at in range(3))
    fs, i_s, us = (sin_part[at * sub : (at + 1) * sub] for at in range(3))
    cc = [fc * ic, fc * uc, uc * ic]
    ss = [fs * i_s, fs * us, us * i_s]
    new_cos = [cc[0] - ss[0], cc[1] + ss[1], cc[2] + ss[2]]
    new_sin = [fc * i_s + fs * ic, fc * us - fs * uc, us * ic - uc * i_s]
    new_cos = jnp.concatenate(new_cos, axis=0)
    new_sin = jnp.concatenate(new_sin, axis=0)
    if first:
        lane = lax.broadcasted_iota(jnp.int32, new_cos.shape, 1) == 0
        new_cos = jnp.where(lane, 0.5 * jnp.concatenate(cc, axis=0), new_cos)
        new_sin = jnp.where(lane, 0.5 * jnp.concatenate(ss, axis=0), new_sin)
    return jnp.concatenate([new_cos, new_sin], axis=1)


def convolve(pieces, high_ref, low_ref, turn_ref, sub):
    blocks = len(pieces)
    block = pieces[0].shape[1]
    rows = 3 * sub
    scale = 1.0 / (blocks * block)
    turns = [(turn_ref[at : at + 1], turn_ref[blocks + at : blocks + at + 1]) for at in range(blocks)]
    first = dot_both(jnp.concatenate(fold(pieces, 0, blocks), axis=1), high_ref[0], low_ref[0])
    packed = []
    for residue in range(1, blocks):
        even, odd = fold(pieces, residue, blocks)
        cosine, sine = turns[residue]
        packed.append(
            jnp.concatenate([even * cosine - odd * sine, even * sine + odd * cosine], axis=1)
        )
    spectrum = dot_both(jnp.concatenate(packed, axis=0), high_ref[1], low_ref[1])
    joined = [
        combine(spectrum[at * rows : (at + 1) * rows], block, sub, False) * scale
        for at in range(blocks - 1)
    ]
    head = dot_both(combine(first, block, sub, True) * scale, high_ref[0], low_ref[0], NT)
    back = dot_both(jnp.concatenate(joined, axis=0), high_ref[1], low_ref[1], NT)
    cosines, sines = phases(0, blocks)
    results = [
        weighted([head[:, :block], head[:, block:]], [cosines[at], sines[at]])
        for at in range(blocks)
    ]
    for residue in range(1, blocks):
        real = back[(residue - 1) * rows : residue * rows, :block]
        imag = back[(residue - 1) * rows : residue * rows, block:]
        cosine, sine = turns[residue]
        cosines, sines = phases(residue, blocks)
        pair = [real * cosine + imag * sine, imag * cosine - real * sine]
        for at in range(blocks):
            results[at] = results[at] + weighted(pair, [cosines[at], sines[at]])
    return results


def partners(count):
    spot = lax.axis_index("red")
    return spot + 1 - 2 * lax.rem(spot, 2), count - 1 - spot


def greet(devices, count):
    me = lax.axis_index("seq")
    barrier = pltpu.get_barrier_semaphore()
    for step in range(1, devices):
        peer = lax.rem(me + step, devices)
        pl.semaphore_signal(barrier, inc=1, device_id={"seq": peer}, device_id_type=MESH)
    for partner in partners(count):
        pl.semaphore_signal(barrier, inc=1, device_id={"red": partner}, device_id_type=MESH)


def meet(devices, count):
    pl.semaphore_wait(pltpu.get_barrier_semaphore(), devices - 1 + len(partners(count)))


def remote(source, target, send_sem, recv_sem, **where):
    return pltpu.make_async_remote_copy(
        src_ref=source,
        dst_ref=target,
        send_sem=send_sem,
        recv_sem=recv_sem,
        device_id=where,
        device_id_type=MESH,
    )


def exchange(devices, source, target, send_sem, recv_sem):
    me = lax.axis_index("seq")
    for step in range(1, devices):
        peer = lax.rem(me + step, devices)
        remote(source(peer), target(me), send_sem, recv_sem, seq=peer).start()


def semaphores(chunks, count):
    counts = {
        "load": 7 + count, "signals": 2, "answers": 2, "reduce": 1, "gather": 1,
        "same0": chunks * PIECES, "same1": chunks, "same2": chunks * PIECES,
        "cross0": chunks * PIECES, "cross1": chunks,
        "near": chunks * PIECES, "far": chunks * PIECES, "relay": chunks,
    }
    bases, total = {}, 0
    for name, needed in counts.items():
        bases[name] = total
        total += needed
    return bases, total


def chunk_sizes(piece):
    return [piece * share // sum(SHARES) for share in SHARES]


def main_kernel(
    devices, count, scale_factor,
    tok_hbm, emb_hbm, wt_hbm, filt_hbm, cot_hbm, high_hbm, low_hbm, turn_hbm,
    out_ref, fgrad_ref, grads_ref, weight_ref,
    tok_ref, emb_ref, wt_ref, filt_ref, cot_ref, high_ref, low_ref, turn_ref,
    part, from_same, from_cross, all_ref, out_sig, sig, sending, recv, one_hot,
    sems,
):
    me = lax.axis_index("seq")
    spot = lax.axis_index("red")
    branches, _, piece, _ = wt_ref.shape
    tok_count, width = filt_ref.shape
    vocabulary = emb_ref.shape[0]
    sizes = chunk_sizes(piece)
    starts = [sum(sizes[:at]) for at in range(len(sizes))]
    chunks = len(sizes)
    last = count - 1
    same, cross = partners(count)
    bases, _ = semaphores(chunks, count)

    def sem(name, index=0):
        return sems.at[bases[name] + index]

    low_half = spot * 2 < count
    end = jnp.where(low_half, 0, last)
    middle = jnp.where(low_half, 1, last - 1)
    far_middle = last - middle
    far_end = last - end
    outer = spot == end
    inner = spot == middle
    greet(devices, count)

    def pick(at_end, at_middle):
        return jnp.where(outer, at_end, at_middle)

    orders = [
        pick(far_middle if REDUCE_DIRECT[0] else far_end, far_end),
        pick(far_end if REDUCE_DIRECT[0] else far_middle, far_middle),
        pick(middle, end),
        spot,
    ]

    def goal_at(index):
        return orders[index]

    def load(index, source, target):
        copy = pltpu.make_async_copy(source, target, sem("load", index))
        copy.start()
        return copy

    emb_load = load(0, emb_hbm, emb_ref)
    wt_loads = []
    for index in range(count):
        goal = goal_at(index)
        wt_loads.append(load(7 + index, wt_hbm.at[:, goal], wt_ref.at[:, goal]))
    signal_loads = [
        load(1, filt_hbm, filt_ref), load(2, cot_hbm, cot_ref), load(3, tok_hbm, tok_ref),
    ]
    table_loads = [
        load(4, high_hbm, high_ref), load(5, low_hbm, low_ref), load(6, turn_hbm, turn_ref),
    ]
    def view(ref, chunk, group, at=None):
        rows = branches * sizes[chunk]
        base = branches * starts[chunk]
        if at is not None:
            rows //= PIECES
            base += at * rows
        return ref.at[group, pl.ds(base, rows)]

    def slot(name, chunk, at):
        if name in ("same1", "cross1", "relay"):
            return sem(name, chunk)
        return sem(name, chunk * PIECES + at)

    def to_same(kind, chunk, group, at=None):
        return remote(
            view(part, chunk, group, at), view(from_same, chunk, group, at),
            sem("reduce"), slot(f"same{kind}", chunk, at), red=same,
        )

    def to_cross(kind, chunk, group, at=None):
        return remote(
            view(part, chunk, group, at), view(from_cross, chunk, group, at),
            sem("reduce"), slot(f"cross{kind}", chunk, at), red=cross,
        )

    def share_to(name, chunk, group, at, partner):
        block = view(all_ref, chunk, group, at)
        return remote(block, block, sem("gather"), slot(name, chunk, at), red=partner)

    def every(make, kind, chunk, group):
        for at in range(PIECES):
            make(kind, chunk, group, at).start()

    def add(source, chunk, group, at):
        piece_ref = view(part, chunk, group, at)
        piece_ref[...] = piece_ref[...] + view(source, chunk, group, at)[...]

    def products(index):
        goal = goal_at(index)
        wt_loads[index].wait()
        rows = jnp.concatenate([wt_ref[b, goal] for b in range(branches)], axis=0)
        product = dot(rows, emb_ref[...], NT)
        for start, size in zip(starts, sizes):
            for b in range(branches):
                base = branches * start + b * size
                part[goal, base : base + size] = product[b * piece + start : b * piece + start + size]

    def first_sends(chunk, index):
        direct = REDUCE_DIRECT[chunk]
        if index == 0:
            @pl.when(outer)
            def _():
                if direct:
                    every(to_same, 0, chunk, far_middle)
                else:
                    every(to_same, 2, chunk, far_end)

            if direct:
                @pl.when(inner)
                def _():
                    every(to_cross, 0, chunk, far_end)

        if index == 1:
            @pl.when(outer)
            def _():
                if direct:
                    every(to_cross, 0, chunk, far_end)
                else:
                    every(to_same, 0, chunk, far_middle)

        if index == 2:
            @pl.when(outer)
            def _():
                every(to_same, 1, chunk, middle)

    def pass_far(chunk, at):
        to_same(2, chunk, far_end, at).wait_recv()
        add(from_same, chunk, far_end, at)
        to_cross(0, chunk, far_end, at).start()

    def pass_cross(chunk, at):
        to_same(0, chunk, far_middle, at).wait_recv()
        add(from_same, chunk, far_middle, at)
        to_cross(1, chunk, far_middle, at).start()

    def pass_same(chunk, at):
        to_cross(0, chunk, end, at).wait_recv()
        add(from_cross, chunk, end, at)
        to_same(0, chunk, end, at).start()

    def arrive(chunk):
        @pl.when(inner)
        def _():
            to_same(1, chunk, spot).wait_recv()
            to_cross(1, chunk, spot).wait_recv()

        @pl.when(outer)
        def _():
            for at in range(PIECES):
                to_same(0, chunk, spot, at).wait_recv()
                if REDUCE_DIRECT[chunk]:
                    to_cross(0, chunk, spot, at).wait_recv()

        own = view(part, chunk, spot)[...] + view(from_same, chunk, spot)[...]
        crossed = view(from_cross, chunk, spot)
        if REDUCE_DIRECT[chunk]:
            return own + crossed[...]

        @pl.when(outer)
        def _():
            crossed[...] = jnp.zeros(crossed.shape, jnp.float32)

        return own + crossed[...]

    def share(chunk):
        def near():
            for at in range(PIECES):
                share_to("near", chunk, spot, at, same).start()

        def far():
            for at in range(PIECES):
                share_to("far", chunk, spot, at, cross).start()

        if chunk in FARFIRST:
            far()
            near()
        else:
            near()
            far()

    def relay_same(chunk, at):
        share_to("far", chunk, far_middle, at, cross).wait_recv()
        share_to("relay", chunk, far_middle, at, same).start()

    def relay_cross(chunk, at):
        share_to("near", chunk, end, at, same).wait_recv()
        share_to("relay", chunk, end, at, cross).start()

    def collect(name, group, role):
        @pl.when(role)
        def _():
            for chunk in range(chunks):
                for at in [None] if name == "relay" else range(PIECES):
                    share_to(name, chunk, group, at, same).wait_recv()

    def weights(group):
        product = dot_split(all_ref[group], emb_ref[...]) * scale_factor
        for start, size in zip(starts, sizes):
            for b in range(branches):
                base = branches * start + b * size
                weight_ref[b, group, start : start + size] = product[base : base + size]

    def signal_rows(start, rows, at):
        return sig[at, start : start + rows]

    def channels(chunk, own, hook):
        start, size = starts[chunk], sizes[chunk]
        projected = dot_split(own, one_hot[...])
        pieces = []
        held = []
        for at in range(devices):
            block = projected[:, at * tok_count : (at + 1) * tok_count]
            queries, key_rows, value_rows = (block[b * size : (b + 1) * size] for b in range(3))
            cotangent = signal_rows(piece + start, size, at)
            held.append((queries, key_rows, value_rows, cotangent))
            pieces.append(
                jnp.concatenate(
                    [signal_rows(start, size, at), key_rows * value_rows, cotangent * queries], axis=0
                )
            )
        results = convolve(pieces, high_ref, low_ref, turn_ref, size)
        hook()
        rounded = []
        for at in range(devices):
            queries, key_rows, value_rows, cotangent = held[at]
            conv = results[at][:size]
            grad_inner = results[at][size : 2 * size]
            grads = jnp.concatenate(
                [cotangent * conv, grad_inner * value_rows, grad_inner * key_rows], axis=0
            ).astype(jnp.bfloat16)
            rounded.append(grads)
            base = 5 * start
            sending[at, base : base + size] = queries * conv
            sending[at, base + size : base + 2 * size] = results[at][2 * size :] * scale_factor
            sending[at, base + 2 * size : base + 5 * size] = grads.astype(jnp.float32)
        sums = dot(jnp.concatenate(rounded, axis=1), one_hot[...], NT)
        view(all_ref, chunk, spot)[...] = sums

    def positions(at):
        parts = [
            recv[peer, 5 * start + at * size : 5 * start + (at + 1) * size]
            for peer in range(devices)
            for start, size in zip(starts, sizes)
        ]
        return jnp.concatenate(parts, axis=0).T

    emb_load.wait()
    products(0)
    meet(devices, count)
    first_sends(0, 0)
    for copy in signal_loads:
        copy.wait()
    filt_t = filt_ref[...].T
    cot_t = cot_ref[...].T
    tok_rows = jnp.broadcast_to(tok_ref[...].astype(jnp.float32), (8, tok_count))
    for peer in range(devices):
        out_sig[peer, :piece] = filt_t[peer * piece : (peer + 1) * piece]
        out_sig[peer, piece : 2 * piece] = cot_t[peer * piece : (peer + 1) * piece]
        out_sig[peer, 2 * piece :] = tok_rows
    exchange(devices, out_sig.at.__getitem__, sig.at.__getitem__, sem("signals"), sem("signals", 1))
    for index in range(1, count):
        products(index)
        first_sends(0, index)
    for index in ((0, 2, 1) if ORDERB else (0, 1, 2)):
        first_sends(1, index)
    sig[me] = out_sig[me]
    others = pl.ds(0, devices - 1)
    signals = remote(out_sig.at[others], sig.at[others], sem("signals"), sem("signals", 1), red=same)
    answers = remote(sending.at[others], recv.at[others], sem("answers"), sem("answers", 1), red=same)

    @pl.when(inner)
    def _():
        if REDUCE_DIRECT[0]:
            for at in range(PIECES):
                pass_cross(0, at)
                pass_same(0, at)
        else:
            for at in range(PIECES):
                pass_far(0, at)
            if STAGE:
                for at in range(PIECES):
                    pass_cross(0, at)
                for at in range(PIECES):
                    pass_same(0, at)
            else:
                for at in range(PIECES):
                    pass_same(0, at)
                    pass_cross(0, at)
        if REDUCE_DIRECT[1]:
            for at in range(PIECES):
                pass_same(1, at)

    signals.wait_recv()
    ids = jnp.concatenate([signal_rows(2 * piece, 1, at) for at in range(devices)], axis=1)
    vocab_rows = lax.broadcasted_iota(jnp.int32, (vocabulary, devices * tok_count), 0)
    one_hot[...] = jnp.where(vocab_rows == ids.astype(jnp.int32), 1.0, 0.0).astype(jnp.bfloat16)
    for copy in table_loads:
        copy.wait()

    if EARLY:
        @pl.when(inner)
        def _():
            for at in range(PIECES):
                pass_cross(1, at)

    def reduce_hook():
        if EARLY:
            return

        @pl.when(inner)
        def _():
            if REDUCE_DIRECT[1]:
                for at in range(PIECES):
                    pass_cross(1, at)
            else:
                for at in range(PIECES):
                    pass_far(1, at)

    def gather_hook():
        if HOOK == 'after':
            return

        @pl.when(inner)
        def _():
            for at in range(PIECES):
                relay_same(0, at)

    for chunk, hook in enumerate([reduce_hook, gather_hook]):
        if chunk == 1 and not REDUCE_DIRECT[1]:
            @pl.when(inner)
            def _():
                for at in range(PIECES):
                    pass_same(1, at)
                    pass_cross(1, at)

        channels(chunk, arrive(chunk), hook)
        share(chunk)
        rows = pl.ds(5 * starts[chunk], 5 * sizes[chunk])
        exchange(
            devices,
            lambda peer, rows=rows: sending.at[peer, rows],
            lambda slot, rows=rows: recv.at[slot, rows],
            sem("answers"), sem("answers", 1),
        )
        recv[me, 5 * starts[chunk] : 5 * (starts[chunk] + sizes[chunk])] = sending[
            me, 5 * starts[chunk] : 5 * (starts[chunk] + sizes[chunk])
        ]

    @pl.when(inner)
    def _():
        for at in range(PIECES):
            relay_cross(0, at)
        if HOOK == 'after':
            for at in range(PIECES):
                relay_same(0, at)

    weights(spot)

    @pl.when(inner)
    def _():
        for at in range(PIECES):
            relay_cross(1, at)
            relay_same(1, at)

    answers.wait_recv()
    out_ref[...] = positions(0)
    fgrad_ref[...] = positions(1)
    for branch in range(branches):
        grads_ref[branch] = positions(2 + branch).astype(jnp.bfloat16)
    collect("near", middle, outer)
    weights(pick(middle, end))
    collect("far", far_end, outer)
    weights(pick(far_end, far_middle))
    collect("relay", pick(far_middle, far_end), outer | inner)
    weights(pick(far_middle, far_end))
    reduced = pl.ds(0, last)
    remote(part.at[reduced], from_same.at[reduced], sem("reduce"), sem("same0"), red=same).wait_send()

    @pl.when(outer)
    def _():
        pair = all_ref.at[pl.ds(0, 2)]
        remote(pair, pair, sem("gather"), sem("near"), red=same).wait_send()

    @pl.when(inner)
    def _():
        remote(all_ref, all_ref, sem("gather"), sem("near"), red=same).wait_send()

    signals.wait_send()
    answers.wait_send()


def final_kernel(out_in, fgrad_in, grads_in, weight_in, out_ref, fgrad_ref, grads_ref, weight_ref, sem):
    pairs = [(weight_in, weight_ref), (grads_in, grads_ref), (out_in, out_ref), (fgrad_in, fgrad_ref)]
    copies = [
        pltpu.make_async_copy(source, target, sem.at[index])
        for index, (source, target) in enumerate(pairs)
    ]
    for copy in copies:
        copy.start()
    for copy in copies:
        copy.wait()


def kernel_shards(devices, count, token_ids, embedding, proj_weight, filters, cotangent):
    tok_count, width = filters.shape
    vocabulary, depth = embedding.shape
    _, branches, _, piece = proj_weight.shape
    scale_factor = float(tok_count * devices) ** (-0.5)
    chunks = len(SHARES)
    f32 = jnp.float32
    bf16 = jnp.bfloat16
    dma = pltpu.SemaphoreType.DMA
    weight_t = jnp.transpose(proj_weight, (1, 2, 3, 0))
    high, low, turn = transform_tables(tok_count, devices)
    block = (count, branches * piece, vocabulary)
    message = (devices, 2 * piece + 8, tok_count)
    answer = (devices, 5 * piece, tok_count)
    results = (
        ((tok_count, width), f32),
        ((tok_count, width), f32),
        ((branches, tok_count, width), bf16),
        ((branches, count, piece, depth), f32),
    )
    kept = sum(math.prod(shape) * jnp.dtype(kind).itemsize for shape, kind in results) + 2**17
    held = pl.pallas_call(
        functools.partial(main_kernel, devices, count, scale_factor),
        out_shape=tuple(pltpu.VMEM(shape, kind) for shape, kind in results),
        in_specs=[pl.BlockSpec(memory_space=pltpu.HBM)] * 8,
        out_specs=(VMEM,) * 4,
        scratch_shapes=[
            pltpu.VMEM((1, tok_count), jnp.int32),
            pltpu.VMEM(embedding.shape, bf16),
            pltpu.VMEM(weight_t.shape, bf16),
            pltpu.VMEM(filters.shape, f32),
            pltpu.VMEM(cotangent.shape, f32),
            pltpu.VMEM(high.shape, bf16),
            pltpu.VMEM(low.shape, bf16),
            pltpu.VMEM(turn.shape, f32),
            pltpu.VMEM(block, f32),
            pltpu.VMEM(block, f32),
            pltpu.VMEM(block, f32),
            pltpu.VMEM(block, f32),
            pltpu.VMEM(message, f32),
            pltpu.VMEM(message, f32),
            pltpu.VMEM(answer, f32),
            pltpu.VMEM(answer, f32),
            pltpu.VMEM((vocabulary, devices * tok_count), bf16),
            dma((semaphores(chunks, count)[1],)),
        ],
        compiler_params=pltpu.CompilerParams(
            collective_id=0, has_side_effects=True, vmem_limit_bytes=VMEM_BYTES - kept
        ),
        name="hyena_exchange",
    )(
        token_ids.reshape(1, tok_count), embedding, weight_t, filters, cotangent,
        jnp.asarray(high), jnp.asarray(low), jnp.asarray(turn),
    )
    output, filter_grad, grads, weight = pl.pallas_call(
        final_kernel,
        out_shape=tuple(jax.ShapeDtypeStruct(shape, kind) for shape, kind in results),
        in_specs=[VMEM] * 4,
        out_specs=(pl.BlockSpec(memory_space=pltpu.HBM),) * 4,
        scratch_shapes=[dma((4,))],
        compiler_params=pltpu.CompilerParams(vmem_limit_bytes=2**20),
        name="finish",
    )(*held)
    return (
        output,
        filter_grad,
        jnp.transpose(grads, (1, 0, 2)),
        jnp.transpose(weight, (3, 0, 1, 2)),
    )


def fits_kernels(devices, count, token_ids, embedding, proj_weight, filters):
    tok_count, width = filters.shape
    vocabulary, depth = embedding.shape
    _, branches, red_count, piece = proj_weight.shape
    lanes = (tok_count, vocabulary, depth)
    aligned = all(size % 128 == 0 for size in lanes) and piece % (8 * sum(SHARES)) == 0 and branches * piece % (8 * sum(SHARES) * PIECES) == 0
    one_hot = vocabulary * tok_count * devices * 8
    held = 4 * branches * piece * (4 * count * vocabulary + 2 * count * depth)
    sides = 4 * tok_count * devices * 20 * piece + 16 * vocabulary * depth
    return (
        aligned
        and count == 4
        and branches == 3
        and red_count == count
        and width == devices * piece
        and one_hot + held + sides < 36 * 2**20
    )


def angles(numbers, modulus, direction):
    phase = (numbers % modulus).astype(jnp.float32) * (direction * 2.0 * math.pi / modulus)
    return (jnp.cos(phase), jnp.sin(phase))


def rotate(real_part, imag_part, cosine, sine_part):
    return (real_part * cosine - imag_part * sine_part, real_part * sine_part + imag_part * cosine)


def complex_einsum(formula, matrix, values):
    mat_real, mat_imag = matrix
    val_real, val_imag = values
    real_out = jnp.einsum(formula, mat_real, val_real, precision=precise_mode) - jnp.einsum(
        formula, mat_imag, val_imag, precision=precise_mode
    )
    imag_out = jnp.einsum(formula, mat_real, val_imag, precision=precise_mode) + jnp.einsum(
        formula, mat_imag, val_real, precision=precise_mode
    )
    return (real_out, imag_out)


def factors(length_total):
    first_factor = 1
    for candidate in range(1, math.isqrt(length_total) + 1):
        if length_total % candidate == 0:
            first_factor = candidate
    return (first_factor, length_total // first_factor)


def combine_spectra(spec_real, spec_imag, width):
    filt_re = spec_real[..., :width]
    inner_re = spec_real[..., width : 2 * width]
    up_re = spec_real[..., 2 * width :]
    filt_im = spec_imag[..., :width]
    inner_im = spec_imag[..., width : 2 * width]
    up_im = spec_imag[..., 2 * width :]
    joined_real = jnp.concatenate(
        [
            filt_re * inner_re - filt_im * inner_im,
            filt_re * up_re + filt_im * up_im,
            up_re * inner_re + up_im * inner_im,
        ],
        axis=-1,
    )
    joined_imag = jnp.concatenate(
        [
            filt_re * inner_im + filt_im * inner_re,
            filt_re * up_im - filt_im * up_re,
            up_im * inner_re - up_re * inner_im,
        ],
        axis=-1,
    )
    return (joined_real, joined_imag)


def local_convolve(signals):
    length, branch_count, narrow = signals.shape
    total = 2 * length
    first_factor, second_factor = factors(total)
    flat = signals.reshape(length, branch_count * narrow)
    padded = jnp.concatenate([flat, jnp.zeros_like(flat)], axis=0).reshape(
        first_factor, second_factor, branch_count * narrow
    )
    first_index = jnp.arange(first_factor, dtype=jnp.int32)
    second_index = jnp.arange(second_factor, dtype=jnp.int32)
    cosine, sine_part = angles(first_index[:, None] * first_index[None, :], first_factor, -1.0)
    real_part = jnp.einsum("kn,nbm->kbm", cosine, padded, precision=precise_mode)
    imag_part = jnp.einsum("kn,nbm->kbm", sine_part, padded, precision=precise_mode)
    cosine, sine_part = angles(first_index[:, None] * second_index[None, :], total, -1.0)
    real_part, imag_part = rotate(real_part, imag_part, cosine[:, :, None], sine_part[:, :, None])
    real_part, imag_part = complex_einsum(
        "lb,kbm->klm",
        angles(second_index[:, None] * second_index[None, :], second_factor, -1.0),
        (real_part, imag_part),
    )
    real_part, imag_part = combine_spectra(real_part, imag_part, narrow)
    real_part, imag_part = complex_einsum(
        "bl,klm->kbm",
        angles(second_index[:, None] * second_index[None, :], second_factor, 1.0),
        (real_part, imag_part),
    )
    cosine, sine_part = angles(first_index[:, None] * second_index[None, :], total, 1.0)
    real_part, imag_part = rotate(real_part, imag_part, cosine[:, :, None], sine_part[:, :, None])
    cosine, sine_part = angles(first_index[:, None] * first_index[None, :], first_factor, 1.0)
    result = jnp.einsum("nk,kbm->nbm", cosine, real_part, precision=precise_mode) - jnp.einsum(
        "nk,kbm->nbm", sine_part, imag_part, precision=precise_mode
    )
    result = result.reshape(total, branch_count * narrow)[:length] / total
    return result.reshape(length, branch_count, narrow)


def shards(token_ids, embedding, proj_weight, filters, cotangent):
    tok_count = token_ids.shape[0]
    devices = lax.axis_size("seq")
    count = lax.axis_size("red")
    if fits_kernels(devices, count, token_ids, embedding, proj_weight, filters):
        return kernel_shards(
            devices, count, token_ids, embedding, proj_weight, filters, cotangent
        )
    width = filters.shape[1]
    vocabulary = embedding.shape[0]
    width_rows, branches, red_count, piece = proj_weight.shape
    scale_factor = float(tok_count * devices) ** (-0.5)
    table = jnp.dot(
        embedding,
        proj_weight.reshape(width_rows, branches * red_count * piece),
        preferred_element_type=jnp.float32,
    )
    table = table.reshape(vocabulary, branches, red_count, piece)
    own_table = lax.psum_scatter(table, "red", scatter_dimension=2, tiled=True)
    full_table = lax.all_gather(own_table, "seq", axis=3, tiled=True)
    projected = jnp.take(full_table, token_ids, axis=0)
    projected = projected.reshape(tok_count, branches, width)
    queries = projected[:, 0]
    key_rows = projected[:, 1]
    value_rows = projected[:, 2]
    inner = key_rows * value_rows
    upstream = cotangent * queries
    stacked = jnp.stack([filters, inner, upstream], axis=1)
    whole_length = lax.all_to_all(stacked, "seq", split_axis=2, concat_axis=0, tiled=True)
    results = local_convolve(whole_length)
    returned = lax.all_to_all(results, "seq", split_axis=0, concat_axis=2, tiled=True)
    conv = returned[:, 0]
    grad_inner = returned[:, 1]
    filter_raw = returned[:, 2]
    output = queries * conv
    filter_grad = filter_raw * scale_factor
    branch_grads = jnp.stack(
        [cotangent * conv, grad_inner * value_rows, grad_inner * key_rows], axis=1
    ).astype(jnp.bfloat16)
    one_hot = (token_ids[:, None] == lax.iota(jnp.int32, vocabulary)[None, :]).astype(jnp.bfloat16)
    token_sums = lax.dot_general(
        one_hot,
        branch_grads.reshape(tok_count, branches * width),
        (((0,), (0,)), ((), ())),
        preferred_element_type=jnp.float32,
    )
    summed = lax.psum_scatter(
        token_sums.reshape(vocabulary, branches, width), "seq", scatter_dimension=2, tiled=True
    )
    gathered = lax.all_gather(summed[:, :, None, :], "red", axis=2, tiled=True)
    weight_grad = (
        lax.dot_general(
            embedding.astype(jnp.float32),
            gathered.reshape(vocabulary, branches * red_count * piece),
            (((0,), (0,)), ((), ())),
            precision=precise_mode,
        )
        * scale_factor
    )
    return (
        output,
        filter_grad,
        branch_grads,
        weight_grad.reshape(width_rows, branches, red_count, piece),
    )


def solution(mesh):
    in_specs = (
        P("seq"),
        P(None, "red"),
        P("red", None, None, "seq"),
        P("seq", "red"),
        P("seq", "red"),
    )
    out_specs = (
        P("seq", "red"),
        P("seq", "red"),
        P("seq", None, "red"),
        P("red", None, None, "seq"),
    )
    return jax.shard_map(shards, mesh=mesh, in_specs=in_specs, out_specs=out_specs, check_vma=False)
```

```python
import functools
import math

import jax
import jax.numpy as jnp
import numpy as np
from jax import lax
from jax.experimental import pallas as pl
from jax.experimental.pallas import tpu as pltpu
from jax.sharding import PartitionSpec as P

precise_mode = lax.Precision.HIGHEST
MESH = pl.DeviceIdType.MESH
VMEM = pl.BlockSpec(memory_space=pltpu.VMEM)
SHARES = (1, 1)
REDUCE_DIRECT = (False, True)
EARLY = True
ORDERB = True
STAGE = True
HOOK = 'after'
FARFIRST = ()
PIECES = 3
VMEM_BYTES = 67043328
NN = (((1,), (0,)), ((), ()))
NT = (((1,), (1,)), ((), ()))


def dot(left, right, dims=NN):
    return lax.dot_general(left, right, dims, preferred_element_type=jnp.float32)


def stack_split(value):
    high = value.astype(jnp.bfloat16).astype(jnp.float32)
    return jnp.concatenate([high, value - high], axis=0).astype(jnp.bfloat16)


def dot_split(value, matrix, dims=NN):
    both = dot(stack_split(value), matrix, dims)
    rows = value.shape[0]
    return both[:rows] + both[rows:]


def dot_both(value, matrix_high, matrix_low, dims=NN):
    high = value.astype(jnp.bfloat16)
    return dot_split(value, matrix_high, dims) + dot(high, matrix_low, dims)


def transform_tables(block, blocks):
    total = 2 * blocks * block
    place = np.arange(block)
    half = block // 2
    tables = np.zeros((2, 2 * block, 2 * block))
    even = 2 * np.pi * ((2 * blocks * place[:, None] * np.arange(half)[None, :]) % total) / total
    odd = 2 * np.pi * ((place[:, None] * (blocks + 2 * blocks * np.arange(half))[None, :]) % total) / total
    tables[0, :block, :half] = np.cos(even)
    tables[0, :block, block : block + half] = np.sin(even)
    tables[0, :block, block] = 1.0 - 2.0 * (place % 2)
    tables[0, block:, half:block] = np.cos(odd)
    tables[0, block:, block + half :] = np.sin(odd)
    psi = 2 * np.pi * ((place[:, None] * place[None, :]) % block) / block
    tables[1, :block, :block] = np.cos(psi)
    tables[1, :block, block:] = np.sin(psi)
    tables[1, block:, :block] = -np.sin(psi)
    tables[1, block:, block:] = np.cos(psi)
    tables = tables.astype(np.float32)
    high = tables.astype(jnp.bfloat16)
    low = (tables - high.astype(np.float32)).astype(jnp.bfloat16)
    alpha = 2 * np.pi * np.arange(blocks)[:, None] * place[None, :] / total
    return high, low, np.concatenate([np.cos(alpha), np.sin(alpha)]).astype(np.float32)


def phases(residue, blocks):
    if residue == 0:
        return [1.0] * blocks, [(-1.0) ** index for index in range(blocks)]
    turn = [math.pi * ((residue * index) % (2 * blocks)) / blocks for index in range(blocks)]
    return [math.cos(a) for a in turn], [math.sin(a) for a in turn]


def weighted(terms, weights):
    total = None
    for term, weight in zip(terms, weights):
        if abs(weight) < 1e-12:
            continue
        part = term if weight == 1.0 else (-term if weight == -1.0 else term * weight)
        total = part if total is None else total + part
    return total


def fold(pieces, residue, blocks, pairs):
    cosines, sines = phases(residue, blocks)
    half = blocks // 2
    if residue == 0 or blocks % 2:
        return weighted(pieces, cosines), weighted(pieces, sines)
    sums, gaps = pairs
    real, imag = (sums, gaps) if residue % 2 == 0 else (gaps, sums)
    at = range(1, half)
    return (
        weighted([pieces[0], pieces[half]] + [real[i] for i in at], [1.0, cosines[half]] + [cosines[i] for i in at]),
        weighted([pieces[half]] + [imag[i] for i in at], [sines[half]] + [sines[i] for i in at]),
    )


def turns_of(turn_ref):
    blocks = turn_ref.shape[0] // 2
    return [(turn_ref[at : at + 1], turn_ref[blocks + at : blocks + at + 1]) for at in range(blocks)]


def forward(pieces, high_ref, low_ref, turn_ref):
    blocks = len(pieces)
    turns = turns_of(turn_ref)
    inside = range(1, blocks // 2)
    pairs = (
        {i: pieces[i] + pieces[blocks - i] for i in inside},
        {i: pieces[i] - pieces[blocks - i] for i in inside},
    )
    first = dot_both(jnp.concatenate(fold(pieces, 0, blocks, pairs), axis=1), high_ref[0], low_ref[0])
    packed = []
    for residue in range(1, blocks):
        even, odd = fold(pieces, residue, blocks, pairs)
        cosine, sine = turns[residue]
        packed.append(
            jnp.concatenate([even * cosine - odd * sine, even * sine + odd * cosine], axis=1)
        )
    return first, dot_both(jnp.concatenate(packed, axis=0), high_ref[1], low_ref[1])


def combine(kernel, spectrum, block, sub, first):
    fc, fs = kernel[:, :block], kernel[:, block:]
    ic, uc = (spectrum[at * sub : (at + 1) * sub, :block] for at in range(2))
    i_s, us = (spectrum[at * sub : (at + 1) * sub, block:] for at in range(2))
    cc = [fc * ic, fc * uc, uc * ic]
    ss = [fs * i_s, fs * us, us * i_s]
    new_cos = [cc[0] - ss[0], cc[1] + ss[1], cc[2] + ss[2]]
    new_sin = [fc * i_s + fs * ic, fc * us - fs * uc, us * ic - uc * i_s]
    new_cos = jnp.concatenate(new_cos, axis=0)
    new_sin = jnp.concatenate(new_sin, axis=0)
    if first:
        lane = lax.broadcasted_iota(jnp.int32, new_cos.shape, 1) == 0
        new_cos = jnp.where(lane, 0.5 * jnp.concatenate(cc, axis=0), new_cos)
        new_sin = jnp.where(lane, 0.5 * jnp.concatenate(ss, axis=0), new_sin)
    return jnp.concatenate([new_cos, new_sin], axis=1)


def convolve(pieces, kernel_first, kernel_rest, high_ref, low_ref, turn_ref, sub):
    blocks = len(pieces)
    block = pieces[0].shape[1]
    rows = 3 * sub
    scale = 1.0 / (blocks * block)
    turns = turns_of(turn_ref)
    first, spectrum = forward(pieces, high_ref, low_ref, turn_ref)
    joined = [
        combine(
            kernel_rest[at * sub : (at + 1) * sub],
            spectrum[at * 2 * sub : (at + 1) * 2 * sub],
            block, sub, False,
        ) * scale
        for at in range(blocks - 1)
    ]
    head = dot_both(combine(kernel_first, first, block, sub, True) * scale, high_ref[0], low_ref[0], NT)
    back = dot_both(jnp.concatenate(joined, axis=0), high_ref[1], low_ref[1], NT)
    cosines, sines = phases(0, blocks)
    results = [
        weighted([head[:, :block], head[:, block:]], [cosines[at], sines[at]])
        for at in range(blocks)
    ]
    half = blocks // 2
    pairs = []
    for residue in range(1, blocks):
        real = back[(residue - 1) * rows : residue * rows, :block]
        imag = back[(residue - 1) * rows : residue * rows, block:]
        cosine, sine = turns[residue]
        pairs.append((real * cosine + imag * sine, imag * cosine - real * sine))
    for at in range(half + 1):
        parts = [[], []]
        for residue in range(1, blocks):
            cosines, sines = phases(residue, blocks)
            real, imag = pairs[residue - 1]
            parts[residue % 2].append((real, cosines[at]))
            parts[1 - residue % 2].append((imag, sines[at]))
        equal, turned = (weighted(*zip(*part)) for part in parts)
        results[at] = results[at] + (equal if turned is None else equal + turned)
        if 0 < at < half:
            results[blocks - at] = results[blocks - at] + (equal - turned)
    return results


def partners(count):
    spot = lax.axis_index("red")
    return spot + 1 - 2 * lax.rem(spot, 2), count - 1 - spot


def greet(devices, count):
    me = lax.axis_index("seq")
    barrier = pltpu.get_barrier_semaphore()
    for step in range(1, devices):
        peer = lax.rem(me + step, devices)
        pl.semaphore_signal(barrier, inc=1, device_id={"seq": peer}, device_id_type=MESH)
    for partner in partners(count):
        pl.semaphore_signal(barrier, inc=1, device_id={"red": partner}, device_id_type=MESH)


def meet(devices, count):
    pl.semaphore_wait(pltpu.get_barrier_semaphore(), devices - 1 + len(partners(count)))


def remote(source, target, send_sem, recv_sem, **where):
    return pltpu.make_async_remote_copy(
        src_ref=source,
        dst_ref=target,
        send_sem=send_sem,
        recv_sem=recv_sem,
        device_id=where,
        device_id_type=MESH,
    )


def exchange(devices, source, target, send_sem, recv_sem):
    me = lax.axis_index("seq")
    for step in range(1, devices):
        peer = lax.rem(me + step, devices)
        remote(source(peer), target(me), send_sem, recv_sem, seq=peer).start()


def semaphores(chunks, count):
    counts = {
        "load": 7 + count, "signals": 2, "answers": 2, "reduce": 1, "gather": 1,
        "same0": chunks * PIECES, "same1": chunks, "same2": chunks * PIECES,
        "cross0": chunks * PIECES, "cross1": chunks,
        "near": chunks * PIECES, "far": chunks * PIECES, "relay": chunks,
    }
    bases, total = {}, 0
    for name, needed in counts.items():
        bases[name] = total
        total += needed
    return bases, total


def chunk_sizes(piece):
    return [piece * share // sum(SHARES) for share in SHARES]


def main_kernel(
    devices, count, scale_factor,
    tok_hbm, emb_hbm, wt_hbm, filt_hbm, cot_hbm, high_hbm, low_hbm, turn_hbm,
    out_ref, fgrad_ref, grads_ref, weight_ref,
    tok_ref, emb_ref, wt_ref, filt_ref, cot_ref, high_ref, low_ref, turn_ref,
    part, from_same, from_cross, all_ref, out_sig, sig, sending, recv, one_hot, spectra,
    sems,
):
    me = lax.axis_index("seq")
    spot = lax.axis_index("red")
    branches, _, piece, _ = wt_ref.shape
    tok_count, width = filt_ref.shape
    vocabulary = emb_ref.shape[0]
    sizes = chunk_sizes(piece)
    starts = [sum(sizes[:at]) for at in range(len(sizes))]
    chunks = len(sizes)
    last = count - 1
    same, cross = partners(count)
    bases, _ = semaphores(chunks, count)

    def sem(name, index=0):
        return sems.at[bases[name] + index]

    low_half = spot * 2 < count
    end = jnp.where(low_half, 0, last)
    middle = jnp.where(low_half, 1, last - 1)
    far_middle = last - middle
    far_end = last - end
    outer = spot == end
    inner = spot == middle
    greet(devices, count)

    def pick(at_end, at_middle):
        return jnp.where(outer, at_end, at_middle)

    orders = [
        pick(far_middle if REDUCE_DIRECT[0] else far_end, far_end),
        pick(far_end if REDUCE_DIRECT[0] else far_middle, far_middle),
        pick(middle, end),
        spot,
    ]

    def goal_at(index):
        return orders[index]

    def load(index, source, target):
        copy = pltpu.make_async_copy(source, target, sem("load", index))
        copy.start()
        return copy

    emb_load = load(0, emb_hbm, emb_ref)
    wt_loads = []
    for index in range(count):
        goal = goal_at(index)
        wt_loads.append(load(7 + index, wt_hbm.at[:, goal], wt_ref.at[:, goal]))
    signal_loads = [
        load(1, filt_hbm, filt_ref), load(2, cot_hbm, cot_ref), load(3, tok_hbm, tok_ref),
    ]
    table_loads = [
        load(4, high_hbm, high_ref), load(5, low_hbm, low_ref), load(6, turn_hbm, turn_ref),
    ]
    def view(ref, chunk, group, at=None):
        rows = branches * sizes[chunk]
        base = branches * starts[chunk]
        if at is not None:
            rows //= PIECES
            base += at * rows
        return ref.at[group, pl.ds(base, rows)]

    def slot(name, chunk, at):
        if name in ("same1", "cross1", "relay"):
            return sem(name, chunk)
        return sem(name, chunk * PIECES + at)

    def to_same(kind, chunk, group, at=None):
        return remote(
            view(part, chunk, group, at), view(from_same, chunk, group, at),
            sem("reduce"), slot(f"same{kind}", chunk, at), red=same,
        )

    def to_cross(kind, chunk, group, at=None):
        return remote(
            view(part, chunk, group, at), view(from_cross, chunk, group, at),
            sem("reduce"), slot(f"cross{kind}", chunk, at), red=cross,
        )

    def share_to(name, chunk, group, at, partner):
        block = view(all_ref, chunk, group, at)
        return remote(block, block, sem("gather"), slot(name, chunk, at), red=partner)

    def every(make, kind, chunk, group):
        for at in range(PIECES):
            make(kind, chunk, group, at).start()

    def add(source, chunk, group, at):
        piece_ref = view(part, chunk, group, at)
        piece_ref[...] = piece_ref[...] + view(source, chunk, group, at)[...]

    def products(index):
        goal = goal_at(index)
        wt_loads[index].wait()
        rows = jnp.concatenate([wt_ref[b, goal] for b in range(branches)], axis=0)
        product = dot(rows, emb_ref[...], NT)
        for start, size in zip(starts, sizes):
            for b in range(branches):
                base = branches * start + b * size
                part[goal, base : base + size] = product[b * piece + start : b * piece + start + size]

    def first_sends(chunk, index):
        direct = REDUCE_DIRECT[chunk]
        if index == 0:
            @pl.when(outer)
            def _():
                if direct:
                    every(to_same, 0, chunk, far_middle)
                else:
                    every(to_same, 2, chunk, far_end)

            if direct:
                @pl.when(inner)
                def _():
                    every(to_cross, 0, chunk, far_end)

        if index == 1:
            @pl.when(outer)
            def _():
                if direct:
                    every(to_cross, 0, chunk, far_end)
                else:
                    every(to_same, 0, chunk, far_middle)

        if index == 2:
            @pl.when(outer)
            def _():
                every(to_same, 1, chunk, middle)

    def pass_far(chunk, at):
        to_same(2, chunk, far_end, at).wait_recv()
        add(from_same, chunk, far_end, at)
        to_cross(0, chunk, far_end, at).start()

    def pass_cross(chunk, at):
        to_same(0, chunk, far_middle, at).wait_recv()
        add(from_same, chunk, far_middle, at)
        to_cross(1, chunk, far_middle, at).start()

    def pass_same(chunk, at):
        to_cross(0, chunk, end, at).wait_recv()
        add(from_cross, chunk, end, at)
        to_same(0, chunk, end, at).start()

    def arrive(chunk):
        @pl.when(inner)
        def _():
            to_same(1, chunk, spot).wait_recv()
            to_cross(1, chunk, spot).wait_recv()

        @pl.when(outer)
        def _():
            for at in range(PIECES):
                to_same(0, chunk, spot, at).wait_recv()
                if REDUCE_DIRECT[chunk]:
                    to_cross(0, chunk, spot, at).wait_recv()

        own = view(part, chunk, spot)[...] + view(from_same, chunk, spot)[...]
        crossed = view(from_cross, chunk, spot)
        if REDUCE_DIRECT[chunk]:
            return own + crossed[...]

        @pl.when(outer)
        def _():
            crossed[...] = jnp.zeros(crossed.shape, jnp.float32)

        return own + crossed[...]

    def share(chunk):
        def near():
            for at in range(PIECES):
                share_to("near", chunk, spot, at, same).start()

        def far():
            for at in range(PIECES):
                share_to("far", chunk, spot, at, cross).start()

        if chunk in FARFIRST:
            far()
            near()
        else:
            near()
            far()

    def relay_same(chunk, at):
        share_to("far", chunk, far_middle, at, cross).wait_recv()
        share_to("relay", chunk, far_middle, at, same).start()

    def relay_cross(chunk, at):
        share_to("near", chunk, end, at, same).wait_recv()
        share_to("relay", chunk, end, at, cross).start()

    def collect(name, group, role):
        @pl.when(role)
        def _():
            for chunk in range(chunks):
                for at in [None] if name == "relay" else range(PIECES):
                    share_to(name, chunk, group, at, same).wait_recv()

    def weights(group):
        product = dot_split(all_ref[group], emb_ref[...]) * scale_factor
        for start, size in zip(starts, sizes):
            for b in range(branches):
                base = branches * start + b * size
                weight_ref[b, group, start : start + size] = product[base : base + size]

    def signal_rows(start, rows, at):
        return sig[at, start : start + rows]

    def transform_filters(chunk):
        start, size = starts[chunk], sizes[chunk]
        pieces = [signal_rows(start, size, at) for at in range(devices)]
        first, rest = forward(pieces, high_ref, low_ref, turn_ref)
        base = devices * start
        spectra[base : base + size] = first
        spectra[base + size : base + devices * size] = rest

    def channels(chunk, own, hook):
        start, size = starts[chunk], sizes[chunk]
        projected = dot_split(own, one_hot[...])
        pieces = []
        held = []
        for at in range(devices):
            block = projected[:, at * tok_count : (at + 1) * tok_count]
            queries, key_rows, value_rows = (block[b * size : (b + 1) * size] for b in range(3))
            cotangent = signal_rows(piece + start, size, at)
            held.append((queries, key_rows, value_rows, cotangent))
            pieces.append(
                jnp.concatenate([key_rows * value_rows, cotangent * queries], axis=0)
            )
        base = devices * start
        kernel_first = spectra[base : base + size]
        kernel_rest = spectra[base + size : base + devices * size]
        results = convolve(
            pieces, kernel_first, kernel_rest, high_ref, low_ref, turn_ref, size
        )
        hook()
        rounded = []
        for at in range(devices):
            queries, key_rows, value_rows, cotangent = held[at]
            conv = results[at][:size]
            grad_inner = results[at][size : 2 * size]
            grads = jnp.concatenate(
                [cotangent * conv, grad_inner * value_rows, grad_inner * key_rows], axis=0
            ).astype(jnp.bfloat16)
            rounded.append(grads)
            base = 5 * start
            sending[at, base : base + size] = queries * conv
            sending[at, base + size : base + 2 * size] = results[at][2 * size :] * scale_factor
            sending[at, base + 2 * size : base + 5 * size] = grads.astype(jnp.float32)
        sums = dot(jnp.concatenate(rounded, axis=1), one_hot[...], NT)
        view(all_ref, chunk, spot)[...] = sums

    def positions(at):
        parts = [
            recv[peer, 5 * start + at * size : 5 * start + (at + 1) * size]
            for peer in range(devices)
            for start, size in zip(starts, sizes)
        ]
        return jnp.concatenate(parts, axis=0).T

    emb_load.wait()
    products(0)
    meet(devices, count)
    first_sends(0, 0)
    for copy in signal_loads:
        copy.wait()
    filt_t = filt_ref[...].T
    cot_t = cot_ref[...].T
    tok_rows = jnp.broadcast_to(tok_ref[...].astype(jnp.float32), (8, tok_count))
    for peer in range(devices):
        out_sig[peer, :piece] = filt_t[peer * piece : (peer + 1) * piece]
        out_sig[peer, piece : 2 * piece] = cot_t[peer * piece : (peer + 1) * piece]
        out_sig[peer, 2 * piece :] = tok_rows
    exchange(devices, out_sig.at.__getitem__, sig.at.__getitem__, sem("signals"), sem("signals", 1))
    for index in range(1, count):
        products(index)
        first_sends(0, index)
    for index in ((0, 2, 1) if ORDERB else (0, 1, 2)):
        first_sends(1, index)
    sig[me] = out_sig[me]
    others = pl.ds(0, devices - 1)
    signals = remote(out_sig.at[others], sig.at[others], sem("signals"), sem("signals", 1), red=same)
    answers = remote(sending.at[others], recv.at[others], sem("answers"), sem("answers", 1), red=same)

    @pl.when(inner)
    def _():
        if REDUCE_DIRECT[0]:
            for at in range(PIECES):
                pass_cross(0, at)
                pass_same(0, at)
        else:
            for at in range(PIECES):
                pass_far(0, at)
            if STAGE:
                for at in range(PIECES):
                    pass_cross(0, at)
                for at in range(PIECES):
                    pass_same(0, at)
            else:
                for at in range(PIECES):
                    pass_same(0, at)
                    pass_cross(0, at)
        if REDUCE_DIRECT[1]:
            for at in range(PIECES):
                pass_same(1, at)

    signals.wait_recv()
    ids = jnp.concatenate([signal_rows(2 * piece, 1, at) for at in range(devices)], axis=1)
    vocab_rows = lax.broadcasted_iota(jnp.int32, (vocabulary, devices * tok_count), 0)
    one_hot[...] = jnp.where(vocab_rows == ids.astype(jnp.int32), 1.0, 0.0).astype(jnp.bfloat16)
    for copy in table_loads:
        copy.wait()
    for chunk in range(chunks):
        transform_filters(chunk)

    if EARLY:
        @pl.when(inner)
        def _():
            for at in range(PIECES):
                pass_cross(1, at)

    def reduce_hook():
        if EARLY:
            return

        @pl.when(inner)
        def _():
            if REDUCE_DIRECT[1]:
                for at in range(PIECES):
                    pass_cross(1, at)
            else:
                for at in range(PIECES):
                    pass_far(1, at)

    def gather_hook():
        if HOOK == 'after':
            return

        @pl.when(inner)
        def _():
            for at in range(PIECES):
                relay_same(0, at)

    for chunk, hook in enumerate([reduce_hook, gather_hook]):
        if chunk == 1 and not REDUCE_DIRECT[1]:
            @pl.when(inner)
            def _():
                for at in range(PIECES):
                    pass_same(1, at)
                    pass_cross(1, at)

        channels(chunk, arrive(chunk), hook)
        share(chunk)
        rows = pl.ds(5 * starts[chunk], 5 * sizes[chunk])
        exchange(
            devices,
            lambda peer, rows=rows: sending.at[peer, rows],
            lambda slot, rows=rows: recv.at[slot, rows],
            sem("answers"), sem("answers", 1),
        )
        recv[me, 5 * starts[chunk] : 5 * (starts[chunk] + sizes[chunk])] = sending[
            me, 5 * starts[chunk] : 5 * (starts[chunk] + sizes[chunk])
        ]

    @pl.when(inner)
    def _():
        for at in range(PIECES):
            relay_cross(0, at)
        if HOOK == 'after':
            for at in range(PIECES):
                relay_same(0, at)

    weights(spot)

    @pl.when(inner)
    def _():
        for at in range(PIECES):
            relay_cross(1, at)
            relay_same(1, at)

    answers.wait_recv()
    out_ref[...] = positions(0)
    fgrad_ref[...] = positions(1)
    for branch in range(branches):
        grads_ref[branch] = positions(2 + branch).astype(jnp.bfloat16)
    collect("near", middle, outer)
    weights(pick(middle, end))
    collect("far", far_end, outer)
    weights(pick(far_end, far_middle))
    collect("relay", pick(far_middle, far_end), outer | inner)
    weights(pick(far_middle, far_end))
    reduced = pl.ds(0, last)
    remote(part.at[reduced], from_same.at[reduced], sem("reduce"), sem("same0"), red=same).wait_send()

    @pl.when(outer)
    def _():
        pair = all_ref.at[pl.ds(0, 2)]
        remote(pair, pair, sem("gather"), sem("near"), red=same).wait_send()

    @pl.when(inner)
    def _():
        remote(all_ref, all_ref, sem("gather"), sem("near"), red=same).wait_send()

    signals.wait_send()
    answers.wait_send()


def final_kernel(out_in, fgrad_in, grads_in, weight_in, out_ref, fgrad_ref, grads_ref, weight_ref, sem):
    pairs = [(weight_in, weight_ref), (grads_in, grads_ref), (out_in, out_ref), (fgrad_in, fgrad_ref)]
    copies = [
        pltpu.make_async_copy(source, target, sem.at[index])
        for index, (source, target) in enumerate(pairs)
    ]
    for copy in copies:
        copy.start()
    for copy in copies:
        copy.wait()


def kernel_shards(devices, count, token_ids, embedding, proj_weight, filters, cotangent):
    tok_count, width = filters.shape
    vocabulary, depth = embedding.shape
    _, branches, _, piece = proj_weight.shape
    scale_factor = float(tok_count * devices) ** (-0.5)
    chunks = len(SHARES)
    f32 = jnp.float32
    bf16 = jnp.bfloat16
    dma = pltpu.SemaphoreType.DMA
    weight_t = jnp.transpose(proj_weight, (1, 2, 3, 0))
    high, low, turn = transform_tables(tok_count, devices)
    block = (count, branches * piece, vocabulary)
    message = (devices, 2 * piece + 8, tok_count)
    answer = (devices, 5 * piece, tok_count)
    results = (
        ((tok_count, width), f32),
        ((tok_count, width), f32),
        ((branches, tok_count, width), bf16),
        ((branches, count, piece, depth), f32),
    )
    kept = sum(math.prod(shape) * jnp.dtype(kind).itemsize for shape, kind in results) + 2**17
    held = pl.pallas_call(
        functools.partial(main_kernel, devices, count, scale_factor),
        out_shape=tuple(pltpu.VMEM(shape, kind) for shape, kind in results),
        in_specs=[pl.BlockSpec(memory_space=pltpu.HBM)] * 8,
        out_specs=(VMEM,) * 4,
        scratch_shapes=[
            pltpu.VMEM((1, tok_count), jnp.int32),
            pltpu.VMEM(embedding.shape, bf16),
            pltpu.VMEM(weight_t.shape, bf16),
            pltpu.VMEM(filters.shape, f32),
            pltpu.VMEM(cotangent.shape, f32),
            pltpu.VMEM(high.shape, bf16),
            pltpu.VMEM(low.shape, bf16),
            pltpu.VMEM(turn.shape, f32),
            pltpu.VMEM(block, f32),
            pltpu.VMEM(block, f32),
            pltpu.VMEM(block, f32),
            pltpu.VMEM(block, f32),
            pltpu.VMEM(message, f32),
            pltpu.VMEM(message, f32),
            pltpu.VMEM(answer, f32),
            pltpu.VMEM(answer, f32),
            pltpu.VMEM((vocabulary, devices * tok_count), bf16),
            pltpu.VMEM((devices * piece, 2 * tok_count), f32),
            dma((semaphores(chunks, count)[1],)),
        ],
        compiler_params=pltpu.CompilerParams(
            collective_id=0, has_side_effects=True, vmem_limit_bytes=VMEM_BYTES - kept
        ),
        name="hyena_exchange",
    )(
        token_ids.reshape(1, tok_count), embedding, weight_t, filters, cotangent,
        jnp.asarray(high), jnp.asarray(low), jnp.asarray(turn),
    )
    output, filter_grad, grads, weight = pl.pallas_call(
        final_kernel,
        out_shape=tuple(jax.ShapeDtypeStruct(shape, kind) for shape, kind in results),
        in_specs=[VMEM] * 4,
        out_specs=(pl.BlockSpec(memory_space=pltpu.HBM),) * 4,
        scratch_shapes=[dma((4,))],
        compiler_params=pltpu.CompilerParams(vmem_limit_bytes=2**20),
        name="finish",
    )(*held)
    return (
        output,
        filter_grad,
        jnp.transpose(grads, (1, 0, 2)),
        jnp.transpose(weight, (3, 0, 1, 2)),
    )


def fits_kernels(devices, count, token_ids, embedding, proj_weight, filters):
    tok_count, width = filters.shape
    vocabulary, depth = embedding.shape
    _, branches, red_count, piece = proj_weight.shape
    lanes = (tok_count, vocabulary, depth)
    aligned = all(size % 128 == 0 for size in lanes) and piece % (8 * sum(SHARES)) == 0 and branches * piece % (8 * sum(SHARES) * PIECES) == 0
    one_hot = vocabulary * tok_count * devices * 8
    held = 4 * branches * piece * (4 * count * vocabulary + 2 * count * depth)
    sides = 4 * tok_count * devices * 20 * piece + 16 * vocabulary * depth
    return (
        aligned
        and count == 4
        and branches == 3
        and red_count == count
        and width == devices * piece
        and devices % 2 == 0
        and one_hot + held + sides < 36 * 2**20
    )


def angles(numbers, modulus, direction):
    phase = (numbers % modulus).astype(jnp.float32) * (direction * 2.0 * math.pi / modulus)
    return (jnp.cos(phase), jnp.sin(phase))


def rotate(real_part, imag_part, cosine, sine_part):
    return (real_part * cosine - imag_part * sine_part, real_part * sine_part + imag_part * cosine)


def complex_einsum(formula, matrix, values):
    mat_real, mat_imag = matrix
    val_real, val_imag = values
    real_out = jnp.einsum(formula, mat_real, val_real, precision=precise_mode) - jnp.einsum(
        formula, mat_imag, val_imag, precision=precise_mode
    )
    imag_out = jnp.einsum(formula, mat_real, val_imag, precision=precise_mode) + jnp.einsum(
        formula, mat_imag, val_real, precision=precise_mode
    )
    return (real_out, imag_out)


def factors(length_total):
    first_factor = 1
    for candidate in range(1, math.isqrt(length_total) + 1):
        if length_total % candidate == 0:
            first_factor = candidate
    return (first_factor, length_total // first_factor)


def combine_spectra(spec_real, spec_imag, width):
    filt_re = spec_real[..., :width]
    inner_re = spec_real[..., width : 2 * width]
    up_re = spec_real[..., 2 * width :]
    filt_im = spec_imag[..., :width]
    inner_im = spec_imag[..., width : 2 * width]
    up_im = spec_imag[..., 2 * width :]
    joined_real = jnp.concatenate(
        [
            filt_re * inner_re - filt_im * inner_im,
            filt_re * up_re + filt_im * up_im,
            up_re * inner_re + up_im * inner_im,
        ],
        axis=-1,
    )
    joined_imag = jnp.concatenate(
        [
            filt_re * inner_im + filt_im * inner_re,
            filt_re * up_im - filt_im * up_re,
            up_im * inner_re - up_re * inner_im,
        ],
        axis=-1,
    )
    return (joined_real, joined_imag)


def local_convolve(signals):
    length, branch_count, narrow = signals.shape
    total = 2 * length
    first_factor, second_factor = factors(total)
    flat = signals.reshape(length, branch_count * narrow)
    padded = jnp.concatenate([flat, jnp.zeros_like(flat)], axis=0).reshape(
        first_factor, second_factor, branch_count * narrow
    )
    first_index = jnp.arange(first_factor, dtype=jnp.int32)
    second_index = jnp.arange(second_factor, dtype=jnp.int32)
    cosine, sine_part = angles(first_index[:, None] * first_index[None, :], first_factor, -1.0)
    real_part = jnp.einsum("kn,nbm->kbm", cosine, padded, precision=precise_mode)
    imag_part = jnp.einsum("kn,nbm->kbm", sine_part, padded, precision=precise_mode)
    cosine, sine_part = angles(first_index[:, None] * second_index[None, :], total, -1.0)
    real_part, imag_part = rotate(real_part, imag_part, cosine[:, :, None], sine_part[:, :, None])
    real_part, imag_part = complex_einsum(
        "lb,kbm->klm",
        angles(second_index[:, None] * second_index[None, :], second_factor, -1.0),
        (real_part, imag_part),
    )
    real_part, imag_part = combine_spectra(real_part, imag_part, narrow)
    real_part, imag_part = complex_einsum(
        "bl,klm->kbm",
        angles(second_index[:, None] * second_index[None, :], second_factor, 1.0),
        (real_part, imag_part),
    )
    cosine, sine_part = angles(first_index[:, None] * second_index[None, :], total, 1.0)
    real_part, imag_part = rotate(real_part, imag_part, cosine[:, :, None], sine_part[:, :, None])
    cosine, sine_part = angles(first_index[:, None] * first_index[None, :], first_factor, 1.0)
    result = jnp.einsum("nk,kbm->nbm", cosine, real_part, precision=precise_mode) - jnp.einsum(
        "nk,kbm->nbm", sine_part, imag_part, precision=precise_mode
    )
    result = result.reshape(total, branch_count * narrow)[:length] / total
    return result.reshape(length, branch_count, narrow)


def shards(token_ids, embedding, proj_weight, filters, cotangent):
    tok_count = token_ids.shape[0]
    devices = lax.axis_size("seq")
    count = lax.axis_size("red")
    if fits_kernels(devices, count, token_ids, embedding, proj_weight, filters):
        return kernel_shards(
            devices, count, token_ids, embedding, proj_weight, filters, cotangent
        )
    width = filters.shape[1]
    vocabulary = embedding.shape[0]
    width_rows, branches, red_count, piece = proj_weight.shape
    scale_factor = float(tok_count * devices) ** (-0.5)
    table = jnp.dot(
        embedding,
        proj_weight.reshape(width_rows, branches * red_count * piece),
        preferred_element_type=jnp.float32,
    )
    table = table.reshape(vocabulary, branches, red_count, piece)
    own_table = lax.psum_scatter(table, "red", scatter_dimension=2, tiled=True)
    full_table = lax.all_gather(own_table, "seq", axis=3, tiled=True)
    projected = jnp.take(full_table, token_ids, axis=0)
    projected = projected.reshape(tok_count, branches, width)
    queries = projected[:, 0]
    key_rows = projected[:, 1]
    value_rows = projected[:, 2]
    inner = key_rows * value_rows
    upstream = cotangent * queries
    stacked = jnp.stack([filters, inner, upstream], axis=1)
    whole_length = lax.all_to_all(stacked, "seq", split_axis=2, concat_axis=0, tiled=True)
    results = local_convolve(whole_length)
    returned = lax.all_to_all(results, "seq", split_axis=0, concat_axis=2, tiled=True)
    conv = returned[:, 0]
    grad_inner = returned[:, 1]
    filter_raw = returned[:, 2]
    output = queries * conv
    filter_grad = filter_raw * scale_factor
    branch_grads = jnp.stack(
        [cotangent * conv, grad_inner * value_rows, grad_inner * key_rows], axis=1
    ).astype(jnp.bfloat16)
    one_hot = (token_ids[:, None] == lax.iota(jnp.int32, vocabulary)[None, :]).astype(jnp.bfloat16)
    token_sums = lax.dot_general(
        one_hot,
        branch_grads.reshape(tok_count, branches * width),
        (((0,), (0,)), ((), ())),
        preferred_element_type=jnp.float32,
    )
    summed = lax.psum_scatter(
        token_sums.reshape(vocabulary, branches, width), "seq", scatter_dimension=2, tiled=True
    )
    gathered = lax.all_gather(summed[:, :, None, :], "red", axis=2, tiled=True)
    weight_grad = (
        lax.dot_general(
            embedding.astype(jnp.float32),
            gathered.reshape(vocabulary, branches * red_count * piece),
            (((0,), (0,)), ((), ())),
            precision=precise_mode,
        )
        * scale_factor
    )
    return (
        output,
        filter_grad,
        branch_grads,
        weight_grad.reshape(width_rows, branches, red_count, piece),
    )


def solution(mesh):
    in_specs = (
        P("seq"),
        P(None, "red"),
        P("red", None, None, "seq"),
        P("seq", "red"),
        P("seq", "red"),
    )
    out_specs = (
        P("seq", "red"),
        P("seq", "red"),
        P("seq", None, "red"),
        P("red", None, None, "seq"),
    )
    return jax.shard_map(shards, mesh=mesh, in_specs=in_specs, out_specs=out_specs, check_vma=False)
```

```python
import functools
import math

import jax
import jax.numpy as jnp
import numpy as np
from jax import lax
from jax.experimental import pallas as pl
from jax.experimental.pallas import tpu as pltpu
from jax.sharding import PartitionSpec as P

precise_mode = lax.Precision.HIGHEST
MESH = pl.DeviceIdType.MESH
VMEM = pl.BlockSpec(memory_space=pltpu.VMEM)
SHARES = (1, 1)
REDUCE_DIRECT = (False, True)
EARLY = True
ORDERB = True
STAGE = True
HOOK = 'after'
FARFIRST = (1,)
PIECES = 3
VMEM_BYTES = 67043328
NN = (((1,), (0,)), ((), ()))
NT = (((1,), (1,)), ((), ()))


def dot(left, right, dims=NN):
    return lax.dot_general(left, right, dims, preferred_element_type=jnp.float32)


def stack_split(value):
    high = value.astype(jnp.bfloat16).astype(jnp.float32)
    return jnp.concatenate([high, value - high], axis=0).astype(jnp.bfloat16)


def dot_split(value, matrix, dims=NN):
    both = dot(stack_split(value), matrix, dims)
    rows = value.shape[0]
    return both[:rows] + both[rows:]


def dot_both(value, matrix_high, matrix_low, dims=NN):
    high = value.astype(jnp.bfloat16)
    return dot_split(value, matrix_high, dims) + dot(high, matrix_low, dims)


def transform_tables(block, blocks):
    total = 2 * blocks * block
    place = np.arange(block)
    half = block // 2
    tables = np.zeros((2, 2 * block, 2 * block))
    even = 2 * np.pi * ((2 * blocks * place[:, None] * np.arange(half)[None, :]) % total) / total
    odd = 2 * np.pi * ((place[:, None] * (blocks + 2 * blocks * np.arange(half))[None, :]) % total) / total
    tables[0, :block, :half] = np.cos(even)
    tables[0, :block, block : block + half] = np.sin(even)
    tables[0, :block, block] = 1.0 - 2.0 * (place % 2)
    tables[0, block:, half:block] = np.cos(odd)
    tables[0, block:, block + half :] = np.sin(odd)
    psi = 2 * np.pi * ((place[:, None] * place[None, :]) % block) / block
    tables[1, :block, :block] = np.cos(psi)
    tables[1, :block, block:] = np.sin(psi)
    tables[1, block:, :block] = -np.sin(psi)
    tables[1, block:, block:] = np.cos(psi)
    tables = tables.astype(np.float32)
    high = tables.astype(jnp.bfloat16)
    low = (tables - high.astype(np.float32)).astype(jnp.bfloat16)
    alpha = 2 * np.pi * np.arange(blocks)[:, None] * place[None, :] / total
    return high, low, np.concatenate([np.cos(alpha), np.sin(alpha)]).astype(np.float32)


def phases(residue, blocks):
    if residue == 0:
        return [1.0] * blocks, [(-1.0) ** index for index in range(blocks)]
    turn = [math.pi * ((residue * index) % (2 * blocks)) / blocks for index in range(blocks)]
    return [math.cos(a) for a in turn], [math.sin(a) for a in turn]


def weighted(terms, weights):
    total = None
    for term, weight in zip(terms, weights):
        if abs(weight) < 1e-12:
            continue
        part = term if weight == 1.0 else (-term if weight == -1.0 else term * weight)
        total = part if total is None else total + part
    return total


def fold(pieces, residue, blocks):
    cosines, sines = phases(residue, blocks)
    return weighted(pieces, cosines), weighted(pieces, sines)


def combine(spectrum, block, sub, first):
    cos_part = spectrum[:, :block]
    sin_part = spectrum[:, block:]
    fc, ic, uc = (cos_part[at * sub : (at + 1) * sub] for at in range(3))
    fs, i_s, us = (sin_part[at * sub : (at + 1) * sub] for at in range(3))
    cc = [fc * ic, fc * uc, uc * ic]
    ss = [fs * i_s, fs * us, us * i_s]
    new_cos = [cc[0] - ss[0], cc[1] + ss[1], cc[2] + ss[2]]
    new_sin = [fc * i_s + fs * ic, fc * us - fs * uc, us * ic - uc * i_s]
    new_cos = jnp.concatenate(new_cos, axis=0)
    new_sin = jnp.concatenate(new_sin, axis=0)
    if first:
        lane = lax.broadcasted_iota(jnp.int32, new_cos.shape, 1) == 0
        new_cos = jnp.where(lane, 0.5 * jnp.concatenate(cc, axis=0), new_cos)
        new_sin = jnp.where(lane, 0.5 * jnp.concatenate(ss, axis=0), new_sin)
    return jnp.concatenate([new_cos, new_sin], axis=1)


def convolve(pieces, high_ref, low_ref, turn_ref, sub):
    blocks = len(pieces)
    block = pieces[0].shape[1]
    rows = 3 * sub
    scale = 1.0 / (blocks * block)
    turns = [(turn_ref[at : at + 1], turn_ref[blocks + at : blocks + at + 1]) for at in range(blocks)]
    first = dot_both(jnp.concatenate(fold(pieces, 0, blocks), axis=1), high_ref[0], low_ref[0])
    packed = []
    for residue in range(1, blocks):
        even, odd = fold(pieces, residue, blocks)
        cosine, sine = turns[residue]
        packed.append(
            jnp.concatenate([even * cosine - odd * sine, even * sine + odd * cosine], axis=1)
        )
    spectrum = dot_both(jnp.concatenate(packed, axis=0), high_ref[1], low_ref[1])
    joined = [
        combine(spectrum[at * rows : (at + 1) * rows], block, sub, False) * scale
        for at in range(blocks - 1)
    ]
    head = dot_both(combine(first, block, sub, True) * scale, high_ref[0], low_ref[0], NT)
    back = dot_both(jnp.concatenate(joined, axis=0), high_ref[1], low_ref[1], NT)
    cosines, sines = phases(0, blocks)
    results = [
        weighted([head[:, :block], head[:, block:]], [cosines[at], sines[at]])
        for at in range(blocks)
    ]
    for residue in range(1, blocks):
        real = back[(residue - 1) * rows : residue * rows, :block]
        imag = back[(residue - 1) * rows : residue * rows, block:]
        cosine, sine = turns[residue]
        cosines, sines = phases(residue, blocks)
        pair = [real * cosine + imag * sine, imag * cosine - real * sine]
        for at in range(blocks):
            results[at] = results[at] + weighted(pair, [cosines[at], sines[at]])
    return results


def partners(count):
    spot = lax.axis_index("red")
    return spot + 1 - 2 * lax.rem(spot, 2), count - 1 - spot


def greet(devices, count):
    me = lax.axis_index("seq")
    barrier = pltpu.get_barrier_semaphore()
    for step in range(1, devices):
        peer = lax.rem(me + step, devices)
        pl.semaphore_signal(barrier, inc=1, device_id={"seq": peer}, device_id_type=MESH)
    for partner in partners(count):
        pl.semaphore_signal(barrier, inc=1, device_id={"red": partner}, device_id_type=MESH)


def meet(devices, count):
    pl.semaphore_wait(pltpu.get_barrier_semaphore(), devices - 1 + len(partners(count)))


def remote(source, target, send_sem, recv_sem, **where):
    return pltpu.make_async_remote_copy(
        src_ref=source,
        dst_ref=target,
        send_sem=send_sem,
        recv_sem=recv_sem,
        device_id=where,
        device_id_type=MESH,
    )


def exchange(devices, source, target, send_sem, recv_sem):
    me = lax.axis_index("seq")
    for step in range(1, devices):
        peer = lax.rem(me + step, devices)
        remote(source(peer), target(me), send_sem, recv_sem, seq=peer).start()


def semaphores(chunks, count):
    counts = {
        "load": 7 + count, "signals": 2, "answers": 2, "reduce": 1, "gather": 1,
        "same0": chunks * PIECES, "same1": chunks, "same2": PIECES,
        "cross0": chunks * PIECES, "cross1": chunks,
        "near": chunks * PIECES, "far": chunks * PIECES, "relay": chunks,
    }
    bases, total = {}, 0
    for name, needed in counts.items():
        bases[name] = total
        total += needed
    return bases, total


def chunk_sizes(piece):
    return [piece * share // sum(SHARES) for share in SHARES]


def main_kernel(
    devices, count, scale_factor,
    tok_hbm, emb_hbm, wt_hbm, filt_hbm, cot_hbm, high_hbm, low_hbm, turn_hbm,
    out_ref, fgrad_ref, grads_ref, weight_ref,
    tok_ref, emb_ref, wt_ref, filt_ref, cot_ref, high_ref, low_ref, turn_ref,
    part, from_same, from_cross, all_ref, out_sig, sig, sending, recv, one_hot,
    sems,
):
    me = lax.axis_index("seq")
    spot = lax.axis_index("red")
    branches, _, piece, _ = wt_ref.shape
    tok_count, width = filt_ref.shape
    vocabulary = emb_ref.shape[0]
    sizes = chunk_sizes(piece)
    starts = [sum(sizes[:at]) for at in range(len(sizes))]
    chunks = len(sizes)
    last = count - 1
    same, cross = partners(count)
    bases, _ = semaphores(chunks, count)

    def sem(name, index=0):
        return sems.at[bases[name] + index]

    low_half = spot * 2 < count
    end = jnp.where(low_half, 0, last)
    middle = jnp.where(low_half, 1, last - 1)
    far_middle = last - middle
    far_end = last - end
    outer = spot == end
    inner = spot == middle
    greet(devices, count)

    def pick(at_end, at_middle):
        return jnp.where(outer, at_end, at_middle)

    orders = [
        pick(far_middle if REDUCE_DIRECT[0] else far_end, far_end),
        pick(far_end if REDUCE_DIRECT[0] else far_middle, far_middle),
        pick(middle, end),
        spot,
    ]

    def goal_at(index):
        return orders[index]

    def load(index, source, target):
        copy = pltpu.make_async_copy(source, target, sem("load", index))
        copy.start()
        return copy

    emb_load = load(0, emb_hbm, emb_ref)
    wt_loads = []
    for index in range(count):
        goal = goal_at(index)
        wt_loads.append(load(7 + index, wt_hbm.at[:, goal], wt_ref.at[:, goal]))
    signal_loads = [
        load(1, filt_hbm, filt_ref), load(2, cot_hbm, cot_ref), load(3, tok_hbm, tok_ref),
    ]
    table_loads = [
        load(4, high_hbm, high_ref), load(5, low_hbm, low_ref), load(6, turn_hbm, turn_ref),
    ]
    def view(ref, chunk, group, at=None):
        rows = branches * sizes[chunk]
        base = branches * starts[chunk]
        if at is not None:
            rows //= PIECES
            base += at * rows
        return ref.at[group, pl.ds(base, rows)]

    def slot(name, chunk, at):
        if name in ("same1", "cross1", "relay"):
            return sem(name, chunk)
        return sem(name, chunk * PIECES + at)

    def to_same(kind, chunk, group, at=None):
        return remote(
            view(part, chunk, group, at), view(from_same, chunk, group, at),
            sem("reduce"), slot(f"same{kind}", chunk, at), red=same,
        )

    def to_cross(kind, chunk, group, at=None):
        return remote(
            view(part, chunk, group, at), view(from_cross, chunk, group, at),
            sem("reduce"), slot(f"cross{kind}", chunk, at), red=cross,
        )

    def share_to(name, chunk, group, at, partner):
        block = view(all_ref, chunk, group, at)
        return remote(block, block, sem("gather"), slot(name, chunk, at), red=partner)

    def every(make, kind, chunk, group):
        for at in range(PIECES):
            make(kind, chunk, group, at).start()

    def add(source, chunk, group, at):
        piece_ref = view(part, chunk, group, at)
        piece_ref[...] = piece_ref[...] + view(source, chunk, group, at)[...]

    def products(index):
        goal = goal_at(index)
        wt_loads[index].wait()
        rows = jnp.concatenate([wt_ref[b, goal] for b in range(branches)], axis=0)
        product = dot(rows, emb_ref[...], NT)
        for start, size in zip(starts, sizes):
            for b in range(branches):
                base = branches * start + b * size
                part[goal, base : base + size] = product[b * piece + start : b * piece + start + size]

    def first_sends(chunk, index):
        direct = REDUCE_DIRECT[chunk]
        if index == 0:
            @pl.when(outer)
            def _():
                if direct:
                    every(to_same, 0, chunk, far_middle)
                else:
                    every(to_same, 2, chunk, far_end)

            if direct:
                @pl.when(inner)
                def _():
                    every(to_cross, 0, chunk, far_end)

        if index == 1:
            @pl.when(outer)
            def _():
                if direct:
                    every(to_cross, 0, chunk, far_end)
                else:
                    every(to_same, 0, chunk, far_middle)

        if index == 2:
            @pl.when(outer)
            def _():
                every(to_same, 1, chunk, middle)

    def pass_far(chunk, at):
        to_same(2, chunk, far_end, at).wait_recv()
        add(from_same, chunk, far_end, at)
        to_cross(0, chunk, far_end, at).start()

    def pass_cross(chunk, at):
        to_same(0, chunk, far_middle, at).wait_recv()
        add(from_same, chunk, far_middle, at)
        to_cross(1, chunk, far_middle, at).start()

    def pass_same(chunk, at):
        to_cross(0, chunk, end, at).wait_recv()
        add(from_cross, chunk, end, at)
        to_same(0, chunk, end, at).start()

    def arrive(chunk):
        @pl.when(inner)
        def _():
            to_same(1, chunk, spot).wait_recv()
            to_cross(1, chunk, spot).wait_recv()

        @pl.when(outer)
        def _():
            for at in range(PIECES):
                to_same(0, chunk, spot, at).wait_recv()
                if REDUCE_DIRECT[chunk]:
                    to_cross(0, chunk, spot, at).wait_recv()

        own = view(part, chunk, spot)[...] + view(from_same, chunk, spot)[...]
        crossed = view(from_cross, chunk, spot)
        if REDUCE_DIRECT[chunk]:
            return own + crossed[...]

        @pl.when(outer)
        def _():
            crossed[...] = jnp.zeros(crossed.shape, jnp.float32)

        return own + crossed[...]

    def share(chunk):
        def near():
            for at in range(PIECES):
                share_to("near", chunk, spot, at, same).start()

        def far():
            for at in range(PIECES):
                share_to("far", chunk, spot, at, cross).start()

        if chunk in FARFIRST:
            far()
            near()
        else:
            near()
            far()

    def relay_same(chunk, at):
        share_to("far", chunk, far_middle, at, cross).wait_recv()
        share_to("relay", chunk, far_middle, at, same).start()

    def relay_cross(chunk, at):
        share_to("near", chunk, end, at, same).wait_recv()
        share_to("relay", chunk, end, at, cross).start()

    def collect(name, group, role):
        @pl.when(role)
        def _():
            for chunk in range(chunks):
                for at in [None] if name == "relay" else range(PIECES):
                    share_to(name, chunk, group, at, same).wait_recv()

    def weights(group):
        product = dot_split(all_ref[group], emb_ref[...]) * scale_factor
        for start, size in zip(starts, sizes):
            for b in range(branches):
                base = branches * start + b * size
                weight_ref[b, group, start : start + size] = product[base : base + size]

    def signal_rows(start, rows, at):
        return sig[at, start : start + rows]

    def channels(chunk, own, hook):
        start, size = starts[chunk], sizes[chunk]
        projected = dot_split(own, one_hot[...])
        pieces = []
        held = []
        for at in range(devices):
            block = projected[:, at * tok_count : (at + 1) * tok_count]
            queries, key_rows, value_rows = (block[b * size : (b + 1) * size] for b in range(3))
            cotangent = signal_rows(piece + start, size, at)
            held.append((queries, key_rows, value_rows, cotangent))
            pieces.append(
                jnp.concatenate(
                    [signal_rows(start, size, at), key_rows * value_rows, cotangent * queries], axis=0
                )
            )
        results = convolve(pieces, high_ref, low_ref, turn_ref, size)
        hook()
        rounded = []
        for at in range(devices):
            queries, key_rows, value_rows, cotangent = held[at]
            conv = results[at][:size]
            grad_inner = results[at][size : 2 * size]
            grads = jnp.concatenate(
                [cotangent * conv, grad_inner * value_rows, grad_inner * key_rows], axis=0
            ).astype(jnp.bfloat16)
            rounded.append(grads)
            base = 5 * start
            sending[at, base : base + size] = queries * conv
            sending[at, base + size : base + 2 * size] = results[at][2 * size :] * scale_factor
            sending[at, base + 2 * size : base + 5 * size] = grads.astype(jnp.float32)
        sums = dot(jnp.concatenate(rounded, axis=1), one_hot[...], NT)
        view(all_ref, chunk, spot)[...] = sums

    def positions(at):
        parts = [
            recv[peer, 5 * start + at * size : 5 * start + (at + 1) * size]
            for peer in range(devices)
            for start, size in zip(starts, sizes)
        ]
        return jnp.concatenate(parts, axis=0).T

    emb_load.wait()
    products(0)
    meet(devices, count)
    first_sends(0, 0)
    for copy in signal_loads:
        copy.wait()
    filt_t = filt_ref[...].T
    cot_t = cot_ref[...].T
    tok_rows = jnp.broadcast_to(tok_ref[...].astype(jnp.float32), (8, tok_count))
    for peer in range(devices):
        out_sig[peer, :piece] = filt_t[peer * piece : (peer + 1) * piece]
        out_sig[peer, piece : 2 * piece] = cot_t[peer * piece : (peer + 1) * piece]
        out_sig[peer, 2 * piece :] = tok_rows
    exchange(devices, out_sig.at.__getitem__, sig.at.__getitem__, sem("signals"), sem("signals", 1))
    for index in range(1, count):
        products(index)
        first_sends(0, index)
    for index in ((0, 2, 1) if ORDERB else (0, 1, 2)):
        first_sends(1, index)
    sig[me] = out_sig[me]
    others = pl.ds(0, devices - 1)
    signals = remote(out_sig.at[others], sig.at[others], sem("signals"), sem("signals", 1), red=same)
    answers = remote(sending.at[others], recv.at[others], sem("answers"), sem("answers", 1), red=same)

    @pl.when(inner)
    def _():
        if REDUCE_DIRECT[0]:
            for at in range(PIECES):
                pass_cross(0, at)
                pass_same(0, at)
        else:
            for at in range(PIECES):
                pass_far(0, at)
            if STAGE:
                for at in range(PIECES):
                    pass_cross(0, at)
                for at in range(PIECES):
                    pass_same(0, at)
            else:
                for at in range(PIECES):
                    pass_same(0, at)
                    pass_cross(0, at)
        if REDUCE_DIRECT[1]:
            for at in range(PIECES):
                pass_same(1, at)

    signals.wait_recv()
    ids = jnp.concatenate([signal_rows(2 * piece, 1, at) for at in range(devices)], axis=1)
    vocab_rows = lax.broadcasted_iota(jnp.int32, (vocabulary, devices * tok_count), 0)
    one_hot[...] = jnp.where(vocab_rows == ids.astype(jnp.int32), 1.0, 0.0).astype(jnp.bfloat16)
    for copy in table_loads:
        copy.wait()

    if EARLY:
        @pl.when(inner)
        def _():
            for at in range(PIECES):
                pass_cross(1, at)

    def reduce_hook():
        if EARLY:
            return

        @pl.when(inner)
        def _():
            if REDUCE_DIRECT[1]:
                for at in range(PIECES):
                    pass_cross(1, at)
            else:
                for at in range(PIECES):
                    pass_far(1, at)

    def gather_hook():
        if HOOK == 'after':
            return

        @pl.when(inner)
        def _():
            for at in range(PIECES):
                relay_same(0, at)

    for chunk, hook in enumerate([reduce_hook, gather_hook]):
        if chunk == 1 and not REDUCE_DIRECT[1]:
            @pl.when(inner)
            def _():
                for at in range(PIECES):
                    pass_same(1, at)
                    pass_cross(1, at)

        channels(chunk, arrive(chunk), hook)
        share(chunk)
        rows = pl.ds(5 * starts[chunk], 5 * sizes[chunk])
        exchange(
            devices,
            lambda peer, rows=rows: sending.at[peer, rows],
            lambda slot, rows=rows: recv.at[slot, rows],
            sem("answers"), sem("answers", 1),
        )
        recv[me, 5 * starts[chunk] : 5 * (starts[chunk] + sizes[chunk])] = sending[
            me, 5 * starts[chunk] : 5 * (starts[chunk] + sizes[chunk])
        ]

    @pl.when(inner)
    def _():
        for at in range(PIECES):
            relay_cross(0, at)
        if HOOK == 'after':
            for at in range(PIECES):
                relay_same(0, at)

    weights(spot)

    @pl.when(inner)
    def _():
        for at in range(PIECES):
            relay_cross(1, at)
            relay_same(1, at)

    answers.wait_recv()
    out_ref[...] = positions(0)
    fgrad_ref[...] = positions(1)
    for branch in range(branches):
        grads_ref[branch] = positions(2 + branch).astype(jnp.bfloat16)
    collect("near", middle, outer)
    weights(pick(middle, end))
    collect("far", far_end, outer)
    weights(pick(far_end, far_middle))
    collect("relay", pick(far_middle, far_end), outer | inner)
    weights(pick(far_middle, far_end))
    reduced = pl.ds(0, last)
    remote(part.at[reduced], from_same.at[reduced], sem("reduce"), sem("same0"), red=same).wait_send()

    @pl.when(outer)
    def _():
        pair = all_ref.at[pl.ds(0, 2)]
        remote(pair, pair, sem("gather"), sem("near"), red=same).wait_send()

    @pl.when(inner)
    def _():
        remote(all_ref, all_ref, sem("gather"), sem("near"), red=same).wait_send()

    signals.wait_send()
    answers.wait_send()


def final_kernel(out_in, fgrad_in, grads_in, weight_in, out_ref, fgrad_ref, grads_ref, weight_ref, sem):
    pairs = [(weight_in, weight_ref), (grads_in, grads_ref), (out_in, out_ref), (fgrad_in, fgrad_ref)]
    copies = [
        pltpu.make_async_copy(source, target, sem.at[index])
        for index, (source, target) in enumerate(pairs)
    ]
    for copy in copies:
        copy.start()
    for copy in copies:
        copy.wait()


def kernel_shards(devices, count, token_ids, embedding, proj_weight, filters, cotangent):
    tok_count, width = filters.shape
    vocabulary, depth = embedding.shape
    _, branches, _, piece = proj_weight.shape
    scale_factor = float(tok_count * devices) ** (-0.5)
    chunks = len(SHARES)
    f32 = jnp.float32
    bf16 = jnp.bfloat16
    dma = pltpu.SemaphoreType.DMA
    weight_t = jnp.transpose(proj_weight, (1, 2, 3, 0))
    high, low, turn = transform_tables(tok_count, devices)
    block = (count, branches * piece, vocabulary)
    message = (devices, 2 * piece + 8, tok_count)
    answer = (devices, 5 * piece, tok_count)
    results = (
        ((tok_count, width), f32),
        ((tok_count, width), f32),
        ((branches, tok_count, width), bf16),
        ((branches, count, piece, depth), f32),
    )
    kept = sum(math.prod(shape) * jnp.dtype(kind).itemsize for shape, kind in results) + 2**17
    held = pl.pallas_call(
        functools.partial(main_kernel, devices, count, scale_factor),
        out_shape=tuple(pltpu.VMEM(shape, kind) for shape, kind in results),
        in_specs=[pl.BlockSpec(memory_space=pltpu.HBM)] * 8,
        out_specs=(VMEM,) * 4,
        scratch_shapes=[
            pltpu.VMEM((1, tok_count), jnp.int32),
            pltpu.VMEM(embedding.shape, bf16),
            pltpu.VMEM(weight_t.shape, bf16),
            pltpu.VMEM(filters.shape, f32),
            pltpu.VMEM(cotangent.shape, f32),
            pltpu.VMEM(high.shape, bf16),
            pltpu.VMEM(low.shape, bf16),
            pltpu.VMEM(turn.shape, f32),
            pltpu.VMEM(block, f32),
            pltpu.VMEM(block, f32),
            pltpu.VMEM(block, f32),
            pltpu.VMEM(block, f32),
            pltpu.VMEM(message, f32),
            pltpu.VMEM(message, f32),
            pltpu.VMEM(answer, f32),
            pltpu.VMEM(answer, f32),
            pltpu.VMEM((vocabulary, devices * tok_count), bf16),
            dma((semaphores(chunks, count)[1],)),
        ],
        compiler_params=pltpu.CompilerParams(
            collective_id=0, has_side_effects=True, vmem_limit_bytes=VMEM_BYTES - kept
        ),
        name="hyena_exchange",
    )(
        token_ids.reshape(1, tok_count), embedding, weight_t, filters, cotangent,
        jnp.asarray(high), jnp.asarray(low), jnp.asarray(turn),
    )
    output, filter_grad, grads, weight = pl.pallas_call(
        final_kernel,
        out_shape=tuple(jax.ShapeDtypeStruct(shape, kind) for shape, kind in results),
        in_specs=[VMEM] * 4,
        out_specs=(pl.BlockSpec(memory_space=pltpu.HBM),) * 4,
        scratch_shapes=[dma((4,))],
        compiler_params=pltpu.CompilerParams(vmem_limit_bytes=2**20),
        name="finish",
    )(*held)
    return (
        output,
        filter_grad,
        jnp.transpose(grads, (1, 0, 2)),
        jnp.transpose(weight, (3, 0, 1, 2)),
    )


def fits_kernels(devices, count, token_ids, embedding, proj_weight, filters):
    tok_count, width = filters.shape
    vocabulary, depth = embedding.shape
    _, branches, red_count, piece = proj_weight.shape
    lanes = (tok_count, vocabulary, depth)
    aligned = all(size % 128 == 0 for size in lanes) and piece % (8 * sum(SHARES)) == 0 and branches * piece % (8 * sum(SHARES) * PIECES) == 0
    one_hot = vocabulary * tok_count * devices * 8
    held = 4 * branches * piece * (4 * count * vocabulary + 2 * count * depth)
    sides = 4 * tok_count * devices * 20 * piece + 16 * vocabulary * depth
    return (
        aligned
        and count == 4
        and branches == 3
        and red_count == count
        and width == devices * piece
        and one_hot + held + sides < 36 * 2**20
    )


def angles(numbers, modulus, direction):
    phase = (numbers % modulus).astype(jnp.float32) * (direction * 2.0 * math.pi / modulus)
    return (jnp.cos(phase), jnp.sin(phase))


def rotate(real_part, imag_part, cosine, sine_part):
    return (real_part * cosine - imag_part * sine_part, real_part * sine_part + imag_part * cosine)


def complex_einsum(formula, matrix, values):
    mat_real, mat_imag = matrix
    val_real, val_imag = values
    real_out = jnp.einsum(formula, mat_real, val_real, precision=precise_mode) - jnp.einsum(
        formula, mat_imag, val_imag, precision=precise_mode
    )
    imag_out = jnp.einsum(formula, mat_real, val_imag, precision=precise_mode) + jnp.einsum(
        formula, mat_imag, val_real, precision=precise_mode
    )
    return (real_out, imag_out)


def factors(length_total):
    first_factor = 1
    for candidate in range(1, math.isqrt(length_total) + 1):
        if length_total % candidate == 0:
            first_factor = candidate
    return (first_factor, length_total // first_factor)


def combine_spectra(spec_real, spec_imag, width):
    filt_re = spec_real[..., :width]
    inner_re = spec_real[..., width : 2 * width]
    up_re = spec_real[..., 2 * width :]
    filt_im = spec_imag[..., :width]
    inner_im = spec_imag[..., width : 2 * width]
    up_im = spec_imag[..., 2 * width :]
    joined_real = jnp.concatenate(
        [
            filt_re * inner_re - filt_im * inner_im,
            filt_re * up_re + filt_im * up_im,
            up_re * inner_re + up_im * inner_im,
        ],
        axis=-1,
    )
    joined_imag = jnp.concatenate(
        [
            filt_re * inner_im + filt_im * inner_re,
            filt_re * up_im - filt_im * up_re,
            up_im * inner_re - up_re * inner_im,
        ],
        axis=-1,
    )
    return (joined_real, joined_imag)


def local_convolve(signals):
    length, branch_count, narrow = signals.shape
    total = 2 * length
    first_factor, second_factor = factors(total)
    flat = signals.reshape(length, branch_count * narrow)
    padded = jnp.concatenate([flat, jnp.zeros_like(flat)], axis=0).reshape(
        first_factor, second_factor, branch_count * narrow
    )
    first_index = jnp.arange(first_factor, dtype=jnp.int32)
    second_index = jnp.arange(second_factor, dtype=jnp.int32)
    cosine, sine_part = angles(first_index[:, None] * first_index[None, :], first_factor, -1.0)
    real_part = jnp.einsum("kn,nbm->kbm", cosine, padded, precision=precise_mode)
    imag_part = jnp.einsum("kn,nbm->kbm", sine_part, padded, precision=precise_mode)
    cosine, sine_part = angles(first_index[:, None] * second_index[None, :], total, -1.0)
    real_part, imag_part = rotate(real_part, imag_part, cosine[:, :, None], sine_part[:, :, None])
    real_part, imag_part = complex_einsum(
        "lb,kbm->klm",
        angles(second_index[:, None] * second_index[None, :], second_factor, -1.0),
        (real_part, imag_part),
    )
    real_part, imag_part = combine_spectra(real_part, imag_part, narrow)
    real_part, imag_part = complex_einsum(
        "bl,klm->kbm",
        angles(second_index[:, None] * second_index[None, :], second_factor, 1.0),
        (real_part, imag_part),
    )
    cosine, sine_part = angles(first_index[:, None] * second_index[None, :], total, 1.0)
    real_part, imag_part = rotate(real_part, imag_part, cosine[:, :, None], sine_part[:, :, None])
    cosine, sine_part = angles(first_index[:, None] * first_index[None, :], first_factor, 1.0)
    result = jnp.einsum("nk,kbm->nbm", cosine, real_part, precision=precise_mode) - jnp.einsum(
        "nk,kbm->nbm", sine_part, imag_part, precision=precise_mode
    )
    result = result.reshape(total, branch_count * narrow)[:length] / total
    return result.reshape(length, branch_count, narrow)


def shards(token_ids, embedding, proj_weight, filters, cotangent):
    tok_count = token_ids.shape[0]
    devices = lax.axis_size("seq")
    count = lax.axis_size("red")
    if fits_kernels(devices, count, token_ids, embedding, proj_weight, filters):
        return kernel_shards(
            devices, count, token_ids, embedding, proj_weight, filters, cotangent
        )
    width = filters.shape[1]
    vocabulary = embedding.shape[0]
    width_rows, branches, red_count, piece = proj_weight.shape
    scale_factor = float(tok_count * devices) ** (-0.5)
    table = jnp.dot(
        embedding,
        proj_weight.reshape(width_rows, branches * red_count * piece),
        preferred_element_type=jnp.float32,
    )
    table = table.reshape(vocabulary, branches, red_count, piece)
    own_table = lax.psum_scatter(table, "red", scatter_dimension=2, tiled=True)
    full_table = lax.all_gather(own_table, "seq", axis=3, tiled=True)
    projected = jnp.take(full_table, token_ids, axis=0)
    projected = projected.reshape(tok_count, branches, width)
    queries = projected[:, 0]
    key_rows = projected[:, 1]
    value_rows = projected[:, 2]
    inner = key_rows * value_rows
    upstream = cotangent * queries
    stacked = jnp.stack([filters, inner, upstream], axis=1)
    whole_length = lax.all_to_all(stacked, "seq", split_axis=2, concat_axis=0, tiled=True)
    results = local_convolve(whole_length)
    returned = lax.all_to_all(results, "seq", split_axis=0, concat_axis=2, tiled=True)
    conv = returned[:, 0]
    grad_inner = returned[:, 1]
    filter_raw = returned[:, 2]
    output = queries * conv
    filter_grad = filter_raw * scale_factor
    branch_grads = jnp.stack(
        [cotangent * conv, grad_inner * value_rows, grad_inner * key_rows], axis=1
    ).astype(jnp.bfloat16)
    one_hot = (token_ids[:, None] == lax.iota(jnp.int32, vocabulary)[None, :]).astype(jnp.bfloat16)
    token_sums = lax.dot_general(
        one_hot,
        branch_grads.reshape(tok_count, branches * width),
        (((0,), (0,)), ((), ())),
        preferred_element_type=jnp.float32,
    )
    summed = lax.psum_scatter(
        token_sums.reshape(vocabulary, branches, width), "seq", scatter_dimension=2, tiled=True
    )
    gathered = lax.all_gather(summed[:, :, None, :], "red", axis=2, tiled=True)
    weight_grad = (
        lax.dot_general(
            embedding.astype(jnp.float32),
            gathered.reshape(vocabulary, branches * red_count * piece),
            (((0,), (0,)), ((), ())),
            precision=precise_mode,
        )
        * scale_factor
    )
    return (
        output,
        filter_grad,
        branch_grads,
        weight_grad.reshape(width_rows, branches, red_count, piece),
    )


def solution(mesh):
    in_specs = (
        P("seq"),
        P(None, "red"),
        P("red", None, None, "seq"),
        P("seq", "red"),
        P("seq", "red"),
    )
    out_specs = (
        P("seq", "red"),
        P("seq", "red"),
        P("seq", None, "red"),
        P("red", None, None, "seq"),
    )
    return jax.shard_map(shards, mesh=mesh, in_specs=in_specs, out_specs=out_specs, check_vma=False)
```
